256 devices in a mesh: band: 64 (over z, x, core), ens: 4 (over y).
Axes of the slice: x: 4, y: 4, z: 8, core: 2. Of those that a mesh axis runs over, the one named last changes fastest.
Arguments:
- grid_latent: bfloat16 [4, 8192, 1024], P('ens', 'band'), may hold values from -6 to 6
- hidden: bfloat16 [4, 2048, 1024], P('ens', 'band'), may hold values from -6 to 6
- d_updated: bfloat16 [4, 2048, 1024], P('ens', 'band'), may hold values from -6 to 6
- w_kv: bfloat16 [1024, 2048], replicated, may hold values from -0.1875 to 0.1875
- w_q: bfloat16 [1024, 1024], replicated, may hold values from -0.1875 to 0.1875
- src_gain: float32 [1024], replicated, may hold values from 0.1 to 1.9
- q_gain: float32 [1024], replicated, may hold values from 0.5 to 40
- src_index: int32 [2048, 12], P('band'), may hold values from 0 to 8191, as said below
- edge_mask: int32 [2048, 12], P('band'), may hold values from 0 to 1, as said below
Outputs:
- updated: bfloat16 [4, 2048, 1024], P('ens', 'band')
- d_grid: bfloat16 [4, 8192, 1024], P('ens', 'band')
- d_wkv_t: float32 [2048, 1024], P(('band', 'ens'))
The draws below stay inside these ranges and needn't reach their ends.
Inputs may be any that keep to these rules, and one draw needn't show every extreme that they name: `src_index`: every edge slot of hidden node h names a grid row from max(0, (h // 32) * 128 - 32) to min(8192, (h // 32 + 1) * 128 + 32) - 1, and in every band both ends of that range are named by a valid edge. `edge_mask`: the first slot of every hidden node is valid.
All inputs are finite; a program needn't handle non-finite values.
Results may differ from the reference program's by a relative error of at most 0.013.
The reference program's roundings to bfloat16 on the way count: a program that leaves them out, or rounds other values in their place, can miss the bound.
Values may be sent and summed in bfloat16 or wider, within the bound.
A program may use at most 128 MiB of HBM per device.

```python
import math
import jax
import jax.numpy as jnp
from jax import lax

D = 1024
HEADS = 16
K = 12
R = 32
G_DEV = 128
H_DEV = 32
MEMBERS = 4
G = 8192
H = 2048
N_BAND = 64


def draw_q_gain(key, part):
    return jax.random.uniform(key, (D,), jnp.float32, 0.5, 1.5)


def draw_src_index(key, part):
    nodes = jnp.arange(H, dtype=jnp.int32)
    band_index = nodes // H_DEV
    lowest = jnp.maximum(band_index * G_DEV - R, 0)
    highest = jnp.minimum((band_index + 1) * G_DEV + R, G)
    picks = jax.random.randint(key, (H, K), lowest[:, None], highest[:, None], dtype=jnp.int32)
    within = nodes % H_DEV
    first_slot = jnp.where(within == 0, lowest, jnp.where(within == 1, highest - 1, picks[:, 0]))
    return picks.at[:, 0].set(first_slot)


def draw_edge_mask(key, part):
    levels = jax.random.randint(key, (H, K), 0, 4, dtype=jnp.int32)
    valid = (levels > 0).astype(jnp.int32)
    return valid.at[:, 0].set(1)


def block_scale(own_key, dims, cuts, least, top_value):
    gain, own = 1.0, jax.random.fold_in(own_key, 6)
    for position, blocks in cuts:
        draws = jnp.exp(jax.random.uniform(jax.random.fold_in(own, position), (blocks,), jnp.float32, least / len(cuts), top_value / len(cuts)))
        gain = gain * jnp.repeat(draws, dims[position] // blocks).reshape([-1 if axis == position else 1 for axis in range(len(dims))])
    return gain


def scatter_about(key, extent, deviation, limit, pieces=(), held_as=jnp.bfloat16):
    drawn = jax.random.normal(key, extent, jnp.float32) * deviation
    if len(pieces) > 0:
        drawn = block_scale(key, extent, pieces, -0.22, 0.18) * drawn
    return jnp.clip(drawn, min=-limit, max=limit).astype(held_as)


def setup_inputs(seed: int = 0) -> dict:
    streams_of = jax.random.split(jax.random.key(seed), 10)
    return {
        "grid_latent": scatter_about(streams_of[0], (MEMBERS, G, D), 1.0, 6.0, ((0, 4), (1, 64))),
        "hidden": scatter_about(streams_of[1], (MEMBERS, H, D), 1.0, 6.0, ((0, 4), (1, 64))),
        "d_updated": scatter_about(streams_of[2], (MEMBERS, H, D), 1.0, 6.0, ((0, 4), (1, 64))),
        "w_kv": scatter_about(streams_of[3], (D, 2 * D), D ** -0.5, 0.1875),
        "w_q": scatter_about(streams_of[4], (D, D), D ** -0.5, 0.1875),
        "src_gain": jnp.clip(1.0 + 0.18 * jax.random.normal(streams_of[5], (D,), jnp.float32), 0.1, 1.9),
        "q_gain": draw_q_gain(jax.random.fold_in(streams_of[9], 71), 0),
        "src_index": draw_src_index(jax.random.fold_in(streams_of[9], 71), 0),
        "edge_mask": draw_edge_mask(jax.random.fold_in(streams_of[9], 71), 0),
    }


EPSILON = 1e-05

def normalize(values):
    values = values.astype(jnp.float32)
    average = lax.optimization_barrier(jnp.mean(values, axis=-1, keepdims=True))
    centred = values - average
    variance = lax.optimization_barrier(jnp.mean(centred * centred, axis=-1, keepdims=True))
    inv_std = lax.rsqrt(variance + EPSILON)
    return (centred * inv_std, inv_std)

def times_transposed(left, right):
    return lax.dot_general(left, right, (((1,), (1,)), ((), ())), preferred_element_type=jnp.float32)

def node_block(queries, hidden_rows, cotangent, kv_window, local_rows, valid_edges):
    node_count, features = queries.shape
    head_dim = features // HEADS
    score_scale = 1.0 / math.sqrt(head_dim)
    highest = lax.Precision.HIGHEST
    gathered = kv_window[local_rows]
    key_rows = gathered[..., :features].reshape(node_count, K, HEADS, head_dim).astype(jnp.float32)
    value_rows = gathered[..., features:].reshape(node_count, K, HEADS, head_dim).astype(jnp.float32)
    query_heads = queries.reshape(node_count, HEADS, head_dim).astype(jnp.float32)
    scores = jnp.einsum('hnd,hknd->hkn', query_heads, key_rows, precision=highest) * score_scale
    valid = valid_edges[:, :, None] > 0
    shifted = jnp.where(valid, scores, -jnp.inf)
    row_max = lax.optimization_barrier(jnp.max(shifted, axis=1, keepdims=True))
    exp_terms = jnp.exp(shifted - row_max)
    attn_probs = exp_terms / lax.optimization_barrier(jnp.sum(exp_terms, axis=1, keepdims=True))
    probs_low = attn_probs.astype(jnp.bfloat16)
    probs_wide = probs_low.astype(jnp.float32)
    attended = jnp.einsum('hkn,hknd->hnd', probs_wide, value_rows, precision=highest)
    attended = attended.reshape(node_count, features)
    updated = (hidden_rows.astype(jnp.float32) + attended).astype(jnp.bfloat16)
    d_wide = cotangent.astype(jnp.float32).reshape(node_count, HEADS, head_dim)
    d_probs = jnp.einsum('hnd,hknd->hkn', d_wide, value_rows, precision=highest)
    d_scores = attn_probs * (d_probs - lax.optimization_barrier(jnp.sum(attn_probs * d_probs, axis=1, keepdims=True)))
    d_keys = d_scores[..., None] * query_heads[:, None] * score_scale
    d_values = probs_wide[..., None] * d_wide[:, None]
    edge_grads = jnp.concatenate([d_keys.reshape(node_count * K, features), d_values.reshape(node_count * K, features)], axis=1)
    partial_value = jnp.zeros((kv_window.shape[0], 2 * features), jnp.float32).at[local_rows.reshape(-1)].add(edge_grads)
    return (updated, partial_value.astype(jnp.bfloat16))

def reference(grid_latent, hidden, d_updated, w_kv, w_q, src_gain, q_gain, src_index, edge_mask):
    features = w_q.shape[0]
    standard, inv_std = normalize(grid_latent)
    gain_wide = src_gain.astype(jnp.float32)
    normed = (standard * gain_wide).astype(jnp.bfloat16)
    kv_all = jnp.dot(normed.reshape(MEMBERS * G, features), w_kv, preferred_element_type=jnp.float32)
    kv_all = kv_all.astype(jnp.bfloat16).reshape(MEMBERS, G, 2 * features)
    kv_padded = jnp.pad(kv_all, ((0, 0), (R, R), (0, 0)))
    normed_padded = jnp.pad(normed, ((0, 0), (R, R), (0, 0)))
    hidden_hat, _ = normalize(hidden)
    hidden_normed = (hidden_hat * q_gain.astype(jnp.float32)).astype(jnp.bfloat16)
    queries = jnp.dot(hidden_normed.reshape(MEMBERS * H, features), w_q, preferred_element_type=jnp.float32)
    queries = queries.astype(jnp.bfloat16).reshape(MEMBERS, H, features)
    window = G_DEV + 2 * R
    zero_index = jnp.zeros((), jnp.int32)

    def one_band(carry, step_index):
        d_padded, d_weights = carry
        member = (step_index // N_BAND).astype(jnp.int32)
        band_index = (step_index % N_BAND).astype(jnp.int32)
        first_row = (band_index * G_DEV).astype(jnp.int32)
        first_node = (band_index * H_DEV).astype(jnp.int32)
        kv_window = lax.dynamic_slice(kv_padded, (member, first_row, zero_index), (1, window, 2 * features))[0]
        normed_window = lax.dynamic_slice(normed_padded, (member, first_row, zero_index), (1, window, features))[0]
        query_rows = lax.dynamic_slice(queries, (member, first_node, zero_index), (1, H_DEV, features))[0]
        hidden_rows = lax.dynamic_slice(hidden, (member, first_node, zero_index), (1, H_DEV, features))[0]
        cotangent = lax.dynamic_slice(d_updated, (member, first_node, zero_index), (1, H_DEV, features))[0]
        local_rows = (lax.dynamic_slice(src_index, (first_node, zero_index), (H_DEV, K)) - (first_row - R)).astype(jnp.int32)
        valid_edges = lax.dynamic_slice(edge_mask, (first_node, zero_index), (H_DEV, K))
        updated_rows, partial_value = node_block(query_rows, hidden_rows, cotangent, kv_window, local_rows, valid_edges)
        d_window = times_transposed(partial_value, w_kv)
        current = lax.dynamic_slice(d_padded, (member, first_row, zero_index), (1, window, features))
        d_padded = lax.dynamic_update_slice(d_padded, current + d_window[None], (member, first_row, zero_index))
        d_weights = d_weights + lax.dot_general(partial_value, normed_window, (((0,), (0,)), ((), ())), preferred_element_type=jnp.float32)
        return ((d_padded, d_weights), updated_rows)
    start_carry = (jnp.zeros((MEMBERS, G + 2 * R, features), jnp.float32), jnp.zeros((2 * features, features), jnp.float32))
    (d_padded, d_weights), updated = lax.scan(one_band, start_carry, jnp.arange(MEMBERS * N_BAND, dtype=jnp.int32))
    updated = updated.reshape(MEMBERS, H, features)
    d_normed = d_padded[:, R:R + G]
    d_scaled = d_normed * gain_wide
    d_grid = inv_std * (d_scaled - lax.optimization_barrier(jnp.mean(d_scaled, axis=-1, keepdims=True)) - standard * lax.optimization_barrier(jnp.mean(d_scaled * standard, axis=-1, keepdims=True)))
    d_wkv_t = d_weights * (1.0 / math.sqrt(MEMBERS * G))
    return (updated, d_grid.astype(jnp.bfloat16), d_wkv_t)
```

```python
import functools
import math

import jax
import jax.numpy as jnp
from jax import lax
from jax.experimental import pallas as pl
from jax.experimental.pallas import tpu as pltpu
from jax.sharding import Mesh
from jax.sharding import PartitionSpec as P

HEADS = 16
K = 12
R = 32
BAND = ("bz", "bx", "bc")
AXES = ("bz", "bx", "bc", "ens")
EPSILON = 1e-05
MESH = pl.DeviceIdType.MESH
F32 = jnp.float32
BF16 = jnp.bfloat16
LANES = 128


def dot(left, right, contract):
    return lax.dot_general(left, right, ((contract[:1], contract[1:]), ((), ())), preferred_element_type=F32)


def normalize(values):
    average = jnp.mean(values, axis=-1, keepdims=True)
    centred = values - average
    variance = jnp.mean(centred * centred, axis=-1, keepdims=True)
    inv_std = lax.rsqrt(variance + EPSILON)
    return centred * inv_std, inv_std


def layer_kernel(
    sizes,
    factor,
    grid_ref,
    hidden_ref,
    cot_ref,
    wkv_hbm,
    wq_hbm,
    src_gain_ref,
    q_gain_ref,
    index_ref,
    mask_ref,
    updated_ref,
    dgrid_ref,
    dw_ref,
    wkv,
    wq,
    standard,
    inv_std,
    win,
    pair_win,
    kv,
    partial,
    parted,
    pair_parted,
    d_norm,
    back_send,
    back_recv,
    send_a,
    recv_a,
    send_b,
    recv_b,
    send_a2,
    recv_a2,
    send_b2,
    recv_b2,
    kept,
    send_z,
    recv_z,
    load_sem,
    halo_send,
    halo_recv,
    pair_send,
    pair_recv,
    back_ssem,
    back_rsem,
    a_ssem,
    a_rsem,
    b_ssem,
    b_rsem,
    a2_ssem,
    a2_rsem,
    b2_ssem,
    b2_rsem,
    z_ssem,
    z_rsem,
):
    nz, nx, ny = sizes
    nb = nz * nx * 2
    rows = grid_ref.shape[0]
    nodes, features = hidden_ref.shape
    window = rows + 2 * R
    half = features // 2
    own = dw_ref.shape[0]

    z, x = lax.axis_index("bz"), lax.axis_index("bx")
    c, y = lax.axis_index("bc"), lax.axis_index("ens")
    band = (z * nx + x) * 2 + c

    def of_band(b):
        return (b // (2 * nx), (b // 2) % nx, b % 2, y)

    below = of_band((band + nb - 1) % nb)
    above = of_band((band + 1) % nb)
    pair = (z, x, 1 - c, y)

    def x_peer(k):
        return (z, (x + k) % nx, c, y)

    def y_peer(k):
        return (z, x, c, (y + k) % ny)

    def z_peer(k):
        return ((z + k) % nz, x, c, y)

    def remote(src, dst, ssem, rsem, device):
        return pltpu.make_async_remote_copy(
            src_ref=src, dst_ref=dst, send_sem=ssem, recv_sem=rsem, device_id=device, device_id_type=MESH
        )

    load_q = pltpu.make_async_copy(wq_hbm, wq, load_sem.at[0])
    load_kv = pltpu.make_async_copy(wkv_hbm, wkv, load_sem.at[1])
    load_q.start()
    load_kv.start()

    barrier = pltpu.get_barrier_semaphore()
    greeted = [below, above]
    greeted += [x_peer(k) for k in range(1, nx)]
    greeted += [y_peer(k) for k in range(1, ny)]
    greeted += [z_peer(k) for k in range(1, nz)]
    for device in greeted:
        pl.semaphore_signal(barrier, inc=1, device_id=device, device_id_type=MESH)

    hat, scale = normalize(grid_ref[...].astype(F32))
    standard[...] = hat
    inv_std[...] = scale
    win[R : R + rows] = (hat * src_gain_ref[...]).astype(BF16)

    pl.semaphore_wait(barrier, len(greeted))

    halo = [
        remote(win.at[R : 2 * R], win.at[R + rows : window], halo_send.at[0], halo_recv.at[0], below),
        remote(win.at[rows : rows + R], win.at[0:R], halo_send.at[1], halo_recv.at[1], above),
    ]
    for copy in halo:
        copy.start()

    hidden_hat, _ = normalize(hidden_ref[...].astype(F32))
    hidden_normed = (hidden_hat * q_gain_ref[...]).astype(BF16)
    load_q.wait()
    score_scale = 1.0 / math.sqrt(features // HEADS)
    queries = (dot(hidden_normed, wq[...], (1, 0)).astype(BF16).astype(F32) * score_scale).astype(BF16)

    local = index_ref[...] - (band * rows - R)
    local = jnp.where(mask_ref[...] > 0, local, -1)
    row_ids = lax.broadcasted_iota(jnp.int32, (nodes, window), 1)
    times = jnp.zeros((nodes, window), F32)
    for j in range(K):
        times = times + jnp.where(local[:, j : j + 1] == row_ids, 1.0, 0.0)
    times = jnp.concatenate([times, times], axis=0)
    live = times > 0.0

    load_kv.wait()
    for copy in halo:
        copy.wait_recv()
    swap_win = remote(win, pair_win, pair_send.at[0], pair_recv.at[0], pair)
    swap_win.start()
    for j in range(4):
        cols = pl.ds(j * half, half)
        kv[:, cols] = dot(win[...], wkv[:, cols], (1, 0)).astype(BF16)

    low_lane = lax.broadcasted_iota(jnp.int32, (nodes, LANES), 1) < features // HEADS
    cot = cot_ref[...]
    zero = jnp.zeros((nodes, LANES), F32)

    def two_heads(block):
        block = block.astype(F32)
        return jnp.concatenate(
            [jnp.where(low_lane, block, zero), jnp.where(low_lane, zero, block)], axis=0
        ).astype(BF16)

    group = ny * own

    def keep_parted(first, tile):
        piece = min(LANES, group)
        for i in range(LANES // piece):
            at, inside = divmod(first + i * piece, group)
            parted[at // (2 * nx), at // 2 % nx, at % 2, inside : inside + piece] = tile[i * piece : (i + 1) * piece]

    for j in range(features // LANES):
        span = slice(j * LANES, (j + 1) * LANES)
        vspan = slice(features + j * LANES, features + (j + 1) * LANES)
        q2 = two_heads(queries[:, span])
        d2 = two_heads(cot[:, span])
        k_rows, v_rows = kv[:, span], kv[:, vspan]
        scores = dot(q2, k_rows, (1, 1))
        d_probs = dot(d2, v_rows, (1, 1))
        shifted = jnp.where(live, scores, -jnp.inf)
        terms = jnp.exp(shifted - jnp.max(shifted, axis=1, keepdims=True))
        probs = terms / jnp.sum(times * terms, axis=1, keepdims=True)
        weights = (times * probs.astype(BF16).astype(F32)).astype(BF16)
        counted = times * probs
        d_scores = (counted * (d_probs - jnp.sum(counted * d_probs, axis=1, keepdims=True))).astype(BF16)
        mixed = dot(weights, v_rows, (1, 0))
        attended = jnp.where(low_lane, mixed[:nodes], mixed[nodes:])
        updated_ref[:, span] = (hidden_ref[:, span].astype(F32) + attended).astype(BF16)
        partial[:, span] = dot(d_scores, q2, (0, 0)).astype(BF16)
        partial[:, vspan] = dot(weights, d2, (0, 0)).astype(BF16)
        keep_parted(j * LANES, dot(q2, d_scores, (0, 0)).astype(BF16))
        keep_parted(features + j * LANES, dot(d2, weights, (0, 0)).astype(BF16))

    swap_part = remote(parted.at[:, :, 1 - c], pair_parted, pair_send.at[1], pair_recv.at[1], pair)
    swap_part.start()
    swap_win.wait()
    swap_part.wait()

    def product(xd, cols):
        mine = jnp.concatenate([parted[i, xd, c] for i in range(nz)], axis=0)
        other = jnp.concatenate([pair_parted[i, xd] for i in range(nz)], axis=0)
        return dot(mine, win[:, cols], (1, 0)) + dot(other, pair_win[:, cols], (1, 0))

    for xd in range(nx):
        tile = product(xd, slice(half, features)).reshape(nz, ny, own, half).astype(BF16)
        for yd in range(ny):
            send_b[yd, :, xd] = tile[:, yd]
    first_b = []
    for k in range(1, ny):
        first_b.append(remote(send_b.at[(y + k) % ny], recv_b.at[k - 1], b_ssem.at[k - 1], b_rsem.at[k - 1], y_peer(k)))
        first_b[-1].start()
    first_a = []
    for k in list(range(1, nx)) + [0]:
        tile = product((x + k) % nx, slice(0, half)).reshape(nz, ny, own, half).astype(BF16)
        send_a[k] = tile
        if k:
            first_a.append(remote(send_a.at[k], recv_a.at[k - 1], a_ssem.at[k - 1], a_rsem.at[k - 1], x_peer(k)))
            first_a[-1].start()

    part = partial[...]
    for j in range(2):
        cols = pl.ds(j * half, half)
        d_norm[:, cols] = dot(part, wkv[cols, :], (1, 1))
    back_send[0] = d_norm[0:R].astype(BF16)
    back_send[1] = d_norm[R + rows : window].astype(BF16)
    back = [
        remote(back_send.at[0], back_recv.at[0], back_ssem.at[0], back_rsem.at[0], below),
        remote(back_send.at[1], back_recv.at[1], back_ssem.at[1], back_rsem.at[1], above),
    ]
    for copy in back:
        copy.start()
    for copy in back:
        copy.wait()
    d_norm[R : 2 * R] += back_recv[1].astype(F32)
    d_norm[rows : rows + R] += back_recv[0].astype(F32)
    dx = d_norm[R : R + rows] * src_gain_ref[...]
    hat = standard[...]
    dgrid_ref[...] = (
        inv_std[...]
        * (dx - jnp.mean(dx, axis=-1, keepdims=True) - hat * jnp.mean(dx * hat, axis=-1, keepdims=True))
    ).astype(BF16)

    for copy in first_b:
        copy.wait()
    second_b = []
    for k in list(range(1, nx)) + [0]:
        xd = (x + k) % nx
        total = send_b[y, :, xd].astype(F32)
        for j in range(ny - 1):
            total = total + recv_b[j, :, xd].astype(F32)
        if k:
            send_b2[k - 1] = total.astype(BF16)
            second_b.append(
                remote(send_b2.at[k - 1], recv_b2.at[k - 1], b2_ssem.at[k - 1], b2_rsem.at[k - 1], x_peer(k))
            )
            second_b[-1].start()
        else:
            kept[:, :, half:] = total
    for copy in first_a:
        copy.wait()
    second_a = []
    for k in list(range(1, ny)) + [0]:
        yd = (y + k) % ny
        total = send_a[0, :, yd].astype(F32)
        for j in range(nx - 1):
            total = total + recv_a[j, :, yd].astype(F32)
        if k:
            send_a2[k - 1] = total.astype(BF16)
            second_a.append(
                remote(send_a2.at[k - 1], recv_a2.at[k - 1], a2_ssem.at[k - 1], a2_rsem.at[k - 1], y_peer(k))
            )
            second_a[-1].start()
        else:
            kept[:, :, :half] = total
    for copy in second_b:
        copy.wait()
    total = kept[:, :, half:]
    for j in range(nx - 1):
        total = total + recv_b2[j].astype(F32)
    send_z[:, :, half:] = total.astype(BF16)
    for copy in second_a:
        copy.wait()
    total = kept[:, :, :half]
    for j in range(ny - 1):
        total = total + recv_a2[j].astype(F32)
    send_z[:, :, :half] = total.astype(BF16)

    third = []
    for k in range(1, nz):
        third.append(
            remote(send_z.at[(z + k) % nz], recv_z.at[k - 1], z_ssem.at[k - 1], z_rsem.at[k - 1], z_peer(k))
        )
        third[-1].start()
    total = send_z[z].astype(F32)
    for k in range(1, nz):
        third[k - 1].wait()
        total = total + recv_z[k - 1].astype(F32)
    dw_ref[...] = total * factor
    for copy in halo:
        copy.wait_send()


def per_device(sizes, grid_latent, hidden, d_updated, w_kv, w_q, src_gain, q_gain, src_index, edge_mask):
    nz, nx, ny = sizes
    _, rows, features = grid_latent.shape
    nodes = hidden.shape[1]
    window = rows + 2 * R
    half = features // 2
    columns = w_kv.shape[1]
    own = columns // (nz * nx * 2 * ny)
    factor = 1.0 / math.sqrt(ny * rows * nz * nx * 2)
    vmem = pl.BlockSpec(memory_space=pltpu.VMEM)
    anywhere = pl.BlockSpec(memory_space=pl.ANY)
    dma = pltpu.SemaphoreType.DMA
    V = pltpu.VMEM
    scratch = [
        V((features, columns), BF16),
        V((features, features), BF16),
        V((rows, features), F32),
        V((rows, 1), F32),
        V((window, features), BF16),
        V((window, features), BF16),
        V((window, columns), BF16),
        V((window, columns), BF16),
        V((nz, nx, 2, ny * own, window), BF16),
        V((nz, nx, ny * own, window), BF16),
        V((window, features), F32),
        V((2, R, features), BF16),
        V((2, R, features), BF16),
        V((nx, nz, ny, own, half), BF16),
        V((nx - 1, nz, ny, own, half), BF16),
        V((ny, nz, nx, own, half), BF16),
        V((ny - 1, nz, nx, own, half), BF16),
        V((ny - 1, nz, own, half), BF16),
        V((ny - 1, nz, own, half), BF16),
        V((nx - 1, nz, own, half), BF16),
        V((nx - 1, nz, own, half), BF16),
        V((nz, own, features), F32),
        V((nz, own, features), BF16),
        V((nz - 1, own, features), BF16),
        dma((2,)),
        dma((2,)),
        dma((2,)),
        dma((2,)),
        dma((2,)),
        dma((2,)),
        dma((2,)),
        dma((nx - 1,)),
        dma((nx - 1,)),
        dma((ny - 1,)),
        dma((ny - 1,)),
        dma((ny - 1,)),
        dma((ny - 1,)),
        dma((nx - 1,)),
        dma((nx - 1,)),
        dma((nz - 1,)),
        dma((nz - 1,)),
    ]
    updated, d_grid, d_wkv_t = pl.pallas_call(
        functools.partial(layer_kernel, sizes, factor),
        out_shape=(
            jax.ShapeDtypeStruct((nodes, features), BF16),
            jax.ShapeDtypeStruct((rows, features), BF16),
            jax.ShapeDtypeStruct((own, features), F32),
        ),
        in_specs=[vmem, vmem, vmem, anywhere, anywhere, vmem, vmem, vmem, vmem],
        out_specs=(vmem, vmem, vmem),
        scratch_shapes=scratch,
        compiler_params=pltpu.CompilerParams(
            collective_id=0, has_side_effects=True, vmem_limit_bytes=52 * 1024 * 1024
        ),
        name="encoder_layer",
    )(
        grid_latent[0],
        hidden[0],
        d_updated[0],
        w_kv,
        w_q,
        src_gain.reshape(1, features),
        q_gain.reshape(1, features),
        src_index,
        edge_mask,
    )
    return (updated[None], d_grid[None], d_wkv_t)


def solution(mesh):
    bands, members = mesh.shape["band"], mesh.shape["ens"]
    nx = 4 if bands >= 64 else 2
    nz = bands // (2 * nx)
    finer = Mesh(mesh.devices.reshape(nz, nx, 2, members), AXES)
    cells = P("ens", BAND, None)
    in_specs = (cells, cells, cells, P(), P(), P(), P(), P(BAND, None), P(BAND, None))
    out_specs = (cells, cells, P(AXES, None))
    return jax.shard_map(
        functools.partial(per_device, (nz, nx, members)),
        mesh=finer,
        in_specs=in_specs,
        out_specs=out_specs,
        check_vma=False,
    )
```

```python
import functools
import math

import jax
import jax.numpy as jnp
from jax import lax
from jax.experimental import pallas as pl
from jax.experimental.pallas import tpu as pltpu
from jax.sharding import Mesh
from jax.sharding import PartitionSpec as P

HEADS = 16
K = 12
R = 32
BAND = ("bz", "bx", "bc")
AXES = ("bz", "bx", "bc", "ens")
EPSILON = 1e-05
MESH = pl.DeviceIdType.MESH
F32 = jnp.float32
BF16 = jnp.bfloat16
LANES = 128


def dot(left, right, contract):
    return lax.dot_general(left, right, ((contract[:1], contract[1:]), ((), ())), preferred_element_type=F32)


def normalize(values):
    average = jnp.mean(values, axis=-1, keepdims=True)
    centred = values - average
    variance = jnp.mean(centred * centred, axis=-1, keepdims=True)
    inv_std = lax.rsqrt(variance + EPSILON)
    return centred * inv_std, inv_std


def layer_kernel(
    sizes,
    factor,
    grid_hbm,
    hidden_hbm,
    cot_hbm,
    wkv_hbm,
    wq_hbm,
    src_gain_hbm,
    q_gain_hbm,
    index_hbm,
    mask_hbm,
    updated_hbm,
    dgrid_hbm,
    dw_hbm,
    updated_ref,
    dgrid_ref,
    dw_ref,
    out_sem,
    grid_ref,
    hidden_ref,
    cot_ref,
    src_gain_ref,
    q_gain_ref,
    index_ref,
    mask_ref,
    edge,
    wkv,
    wq,
    standard,
    inv_std,
    win,
    pair_win,
    kv,
    partial,
    parted,
    pair_parted,
    d_norm,
    back_send,
    back_recv,
    send_a,
    recv_a,
    send_b,
    recv_b,
    send_a2,
    recv_a2,
    send_b2,
    recv_b2,
    kept,
    send_z,
    recv_z,
    load_sem,
    halo_send,
    halo_recv,
    win_send,
    win_recv,
    pair_send,
    pair_recv,
    back_ssem,
    back_rsem,
    a_ssem,
    a_rsem,
    b_ssem,
    b_rsem,
    a2_ssem,
    a2_rsem,
    b2_ssem,
    b2_rsem,
    z_ssem,
    z_rsem,
):
    nz, nx, ny = sizes
    nb = nz * nx * 2
    rows = grid_hbm.shape[0]
    nodes, features = hidden_hbm.shape
    window = rows + 2 * R
    half = features // 2
    own = dw_hbm.shape[0]

    z, x = lax.axis_index("bz"), lax.axis_index("bx")
    c, y = lax.axis_index("bc"), lax.axis_index("ens")
    band = (z * nx + x) * 2 + c

    def of_band(b):
        return (b // (2 * nx), (b // 2) % nx, b % 2, y)

    below = of_band((band + nb - 1) % nb)
    above = of_band((band + 1) % nb)
    pair = (z, x, 1 - c, y)

    def x_peer(k):
        return (z, (x + k) % nx, c, y)

    def y_peer(k):
        return (z, x, c, (y + k) % ny)

    def z_peer(k):
        return ((z + k) % nz, x, c, y)

    def remote(src, dst, ssem, rsem, device):
        return pltpu.make_async_remote_copy(
            src_ref=src, dst_ref=dst, send_sem=ssem, recv_sem=rsem, device_id=device, device_id_type=MESH
        )

    def load(src, dst, i):
        copy = pltpu.make_async_copy(src, dst, load_sem.at[i])
        copy.start()
        return copy

    load_grid = load(grid_hbm, grid_ref, 0)
    load_gain = load(src_gain_hbm, src_gain_ref, 1)
    load_hidden = load(hidden_hbm, hidden_ref, 2)
    load_q_gain = load(q_gain_hbm, q_gain_ref, 3)
    load_q = load(wq_hbm, wq, 4)
    load_index = load(index_hbm, index_ref, 5)
    load_mask = load(mask_hbm, mask_ref, 6)
    quarter = [slice(j * half, (j + 1) * half) for j in range(4)]
    load_kv = [load(wkv_hbm.at[:, cols], wkv.at[:, cols], 8 + j) for j, cols in enumerate(quarter)]
    load_cot = load(cot_hbm, cot_ref, 7)

    barrier = pltpu.get_barrier_semaphore()
    greeted = [below, above]
    greeted += [x_peer(k) for k in range(1, nx)]
    greeted += [y_peer(k) for k in range(1, ny)]
    greeted += [z_peer(k) for k in range(1, nz)]
    for device in greeted:
        pl.semaphore_signal(barrier, inc=1, device_id=device, device_id_type=MESH)

    pl.semaphore_wait(barrier, len(greeted))

    halo = [
        remote(grid_hbm.at[0:R], edge.at[1], halo_send.at[0], halo_recv.at[0], below),
        remote(grid_hbm.at[rows - R : rows], edge.at[0], halo_send.at[1], halo_recv.at[1], above),
    ]
    for copy in halo:
        copy.start()

    load_grid.wait()
    load_gain.wait()
    hat, scale = normalize(grid_ref[...].astype(F32))
    standard[...] = hat
    inv_std[...] = scale
    win[R : R + rows] = (hat * src_gain_ref[...]).astype(BF16)

    load_hidden.wait()
    load_q_gain.wait()
    hidden_hat, _ = normalize(hidden_ref[...].astype(F32))
    hidden_normed = (hidden_hat * q_gain_ref[...]).astype(BF16)
    load_q.wait()
    score_scale = 1.0 / math.sqrt(features // HEADS)
    queries = (dot(hidden_normed, wq[...], (1, 0)).astype(BF16).astype(F32) * score_scale).astype(BF16)

    load_index.wait()
    load_mask.wait()
    local = index_ref[...] - (band * rows - R)
    local = jnp.where(mask_ref[...] > 0, local, -1)
    row_ids = lax.broadcasted_iota(jnp.int32, (window, nodes), 0)
    times = jnp.zeros((window, nodes), F32)
    for j in range(K):
        times = times + jnp.where(local[j : j + 1, :] == row_ids, 1.0, 0.0)
    times = times.T
    times = jnp.concatenate([times, times], axis=0)
    live = times > 0.0

    for j, cols in enumerate(quarter):
        load_kv[j].wait()
        kv[R : R + rows, cols] = dot(win[R : R + rows], wkv[:, cols], (1, 0)).astype(BF16)
    for copy in halo:
        copy.wait_recv()
    hat, _ = normalize(edge[...].reshape(2 * R, features).astype(F32))
    outer = (hat * src_gain_ref[...]).astype(BF16)
    win[0:R] = outer[:R]
    win[R + rows : window] = outer[R:]
    swap_win = remote(win, pair_win, win_send, win_recv, pair)
    swap_win.start()
    for cols in quarter:
        tile = dot(outer, wkv[:, cols], (1, 0)).astype(BF16)
        kv[0:R, cols] = tile[:R]
        kv[R + rows : window, cols] = tile[R:]
    load_cot.wait()

    low_lane = lax.broadcasted_iota(jnp.int32, (nodes, LANES), 1) < features // HEADS
    cot = cot_ref[...]
    zero = jnp.zeros((nodes, LANES), F32)

    def two_heads(block):
        block = block.astype(F32)
        return jnp.concatenate(
            [jnp.where(low_lane, block, zero), jnp.where(low_lane, zero, block)], axis=0
        ).astype(BF16)

    group = ny * own

    swaps = []

    def keep_parted(first, tile):
        piece = min(LANES, group)
        for i in range(LANES // piece):
            at, inside = divmod(first + i * piece, group)
            parted[at % 2, at // (2 * nx), at // 2 % nx, inside : inside + piece, :window] = tile[i * piece : (i + 1) * piece]

    def swap(first, count):
        n = len(swaps)
        swaps.append(
            remote(
                parted.at[1 - c, first : first + count],
                pair_parted.at[first : first + count],
                pair_send.at[n],
                pair_recv.at[n],
                pair,
            )
        )
        swaps[-1].start()

    batches = 2 if nz >= 4 else 1
    blocks = features // LANES
    planes = nz // (2 * batches)
    for j in range(blocks):
        span = slice(j * LANES, (j + 1) * LANES)
        vspan = slice(features + j * LANES, features + (j + 1) * LANES)
        q2 = two_heads(queries[:, span])
        d2 = two_heads(cot[:, span])
        k_rows, v_rows = kv[:, span], kv[:, vspan]
        scores = dot(q2, k_rows, (1, 1))
        d_probs = dot(d2, v_rows, (1, 1))
        shifted = jnp.where(live, scores, -jnp.inf)
        terms = jnp.exp(shifted - jnp.max(shifted, axis=1, keepdims=True))
        probs = terms / jnp.sum(times * terms, axis=1, keepdims=True)
        weights = (times * probs.astype(BF16).astype(F32)).astype(BF16)
        counted = times * probs
        d_scores = (counted * (d_probs - jnp.sum(counted * d_probs, axis=1, keepdims=True))).astype(BF16)
        mixed = dot(weights, v_rows, (1, 0))
        attended = jnp.where(low_lane, mixed[:nodes], mixed[nodes:])
        updated_ref[:, span] = (hidden_ref[:, span].astype(F32) + attended).astype(BF16)
        partial[:, span] = dot(d_scores, q2, (0, 0)).astype(BF16)
        partial[:, vspan] = dot(weights, d2, (0, 0)).astype(BF16)
        keep_parted(j * LANES, dot(q2, d_scores, (0, 0)).astype(BF16))
        keep_parted(features + j * LANES, dot(d2, weights, (0, 0)).astype(BF16))
        if (j + 1) % (blocks // batches) == 0:
            batch = j * batches // blocks
            swap(batch * planes, planes)
            swap(nz // 2 + batch * planes, planes)

    outs = [pltpu.make_async_copy(updated_ref, updated_hbm, out_sem.at[0])]
    outs[0].start()
    swap_win.wait()
    for copy in swaps:
        copy.wait()

    def product(xd, cols):
        mine = jnp.concatenate([parted[c, i, xd, :, :window] for i in range(nz)], axis=0)
        other = jnp.concatenate([pair_parted[i, xd, :, :window] for i in range(nz)], axis=0)
        return dot(mine, win[:, cols], (1, 0)) + dot(other, pair_win[:, cols], (1, 0))

    first_a, first_b = [], []

    def x_first(k):
        send_a[k] = product((x + k) % nx, slice(0, half)).reshape(nz, ny, own, half).astype(BF16)
        if k:
            first_a.append(remote(send_a.at[k], recv_a.at[k - 1], a_ssem.at[k - 1], a_rsem.at[k - 1], x_peer(k)))
            first_a[-1].start()

    x_first(1)
    for xd in range(nx):
        tile = product(xd, slice(half, features)).reshape(nz, ny, own, half).astype(BF16)
        for yd in range(ny):
            send_b[yd, :, xd] = tile[:, yd]
    for k in range(1, ny):
        first_b.append(remote(send_b.at[(y + k) % ny], recv_b.at[k - 1], b_ssem.at[k - 1], b_rsem.at[k - 1], y_peer(k)))
        first_b[-1].start()
    for k in list(range(2, nx)) + [0]:
        x_first(k)

    part = partial[...]
    for j in range(2):
        cols = pl.ds(j * half, half)
        d_norm[:, cols] = dot(part, wkv[cols, :], (1, 1))
    back_send[0] = d_norm[0:R].astype(BF16)
    back_send[1] = d_norm[R + rows : window].astype(BF16)
    back = [
        remote(back_send.at[0], back_recv.at[0], back_ssem.at[0], back_rsem.at[0], below),
        remote(back_send.at[1], back_recv.at[1], back_ssem.at[1], back_rsem.at[1], above),
    ]
    for copy in back:
        copy.start()
    for copy in back:
        copy.wait()
    d_norm[R : 2 * R] += back_recv[1].astype(F32)
    d_norm[rows : rows + R] += back_recv[0].astype(F32)
    dx = d_norm[R : R + rows] * src_gain_ref[...]
    hat = standard[...]
    dgrid_ref[...] = (
        inv_std[...]
        * (dx - jnp.mean(dx, axis=-1, keepdims=True) - hat * jnp.mean(dx * hat, axis=-1, keepdims=True))
    ).astype(BF16)

    outs.append(pltpu.make_async_copy(dgrid_ref, dgrid_hbm, out_sem.at[1]))
    outs[1].start()

    for copy in first_b:
        copy.wait()
    second_b = []
    for k in list(range(1, nx)) + [0]:
        xd = (x + k) % nx
        total = send_b[y, :, xd].astype(F32)
        for j in range(ny - 1):
            total = total + recv_b[j, :, xd].astype(F32)
        if k:
            send_b2[k - 1] = total.astype(BF16)
            second_b.append(
                remote(send_b2.at[k - 1], recv_b2.at[k - 1], b2_ssem.at[k - 1], b2_rsem.at[k - 1], x_peer(k))
            )
            second_b[-1].start()
        else:
            kept[:, :, half:] = total
    for copy in first_a:
        copy.wait()
    second_a = []
    for k in list(range(1, ny)) + [0]:
        yd = (y + k) % ny
        total = send_a[0, :, yd].astype(F32)
        for j in range(nx - 1):
            total = total + recv_a[j, :, yd].astype(F32)
        if k:
            send_a2[k - 1] = total.astype(BF16)
            second_a.append(
                remote(send_a2.at[k - 1], recv_a2.at[k - 1], a2_ssem.at[k - 1], a2_rsem.at[k - 1], y_peer(k))
            )
            second_a[-1].start()
        else:
            kept[:, :, :half] = total
    for copy in second_b:
        copy.wait()
    total = kept[:, :, half:]
    for j in range(nx - 1):
        total = total + recv_b2[j].astype(F32)
    send_z[:, :, half:] = total.astype(BF16)
    for copy in second_a:
        copy.wait()
    total = kept[:, :, :half]
    for j in range(ny - 1):
        total = total + recv_a2[j].astype(F32)
    send_z[:, :, :half] = total.astype(BF16)

    third = []
    for k in range(1, nz):
        third.append(
            remote(send_z.at[(z + k) % nz], recv_z.at[k - 1], z_ssem.at[k - 1], z_rsem.at[k - 1], z_peer(k))
        )
        third[-1].start()
    total = send_z[z].astype(F32)
    for k in range(1, nz):
        third[k - 1].wait()
        total = total + recv_z[k - 1].astype(F32)
    dw_ref[...] = total * factor
    outs.append(pltpu.make_async_copy(dw_ref, dw_hbm, out_sem.at[2]))
    outs[2].start()
    for copy in outs:
        copy.wait()
    for copy in halo:
        copy.wait_send()


def leave_kernel(a, b, c, a_out, b_out, c_out, a_held, b_held, c_held, sem):
    into = [
        pltpu.make_async_copy(src, dst, sem.at[i]) for i, (src, dst) in enumerate([(b, b_held), (a, a_held), (c, c_held)])
    ]
    out = [
        pltpu.make_async_copy(src, dst, sem.at[3 + i])
        for i, (src, dst) in enumerate([(b_held, b_out), (a_held, a_out), (c_held, c_out)])
    ]
    for copy in into:
        copy.start()
    for first, second in zip(into, out):
        first.wait()
        second.start()
    for copy in out:
        copy.wait()


def per_device(sizes, grid_latent, hidden, d_updated, w_kv, w_q, src_gain, q_gain, src_index, edge_mask):
    nz, nx, ny = sizes
    _, rows, features = grid_latent.shape
    nodes = hidden.shape[1]
    window = rows + 2 * R
    half = features // 2
    columns = w_kv.shape[1]
    own = columns // (nz * nx * 2 * ny)
    factor = 1.0 / math.sqrt(ny * rows * nz * nx * 2)
    vmem = pl.BlockSpec(memory_space=pltpu.VMEM)
    hbm = pl.BlockSpec(memory_space=pltpu.HBM)
    dma = pltpu.SemaphoreType.DMA
    V = pltpu.VMEM
    padded = -(-window // LANES) * LANES
    swaps = 4 if nz >= 4 else 2
    scratch = [
        V((nodes, features), BF16),
        V((rows, features), BF16),
        V((own, features), F32),
        dma((3,)),
        V((rows, features), BF16),
        V((nodes, features), BF16),
        V((nodes, features), BF16),
        V((1, features), F32),
        V((1, features), F32),
        V((K, nodes), jnp.int32),
        V((K, nodes), jnp.int32),
        V((2, R, features), BF16),
        V((features, columns), BF16),
        V((features, features), BF16),
        V((rows, features), F32),
        V((rows, 1), F32),
        V((window, features), BF16),
        V((window, features), BF16),
        V((window, columns), BF16),
        V((window, columns), BF16),
        V((2, nz, nx, ny * own, padded), BF16),
        V((nz, nx, ny * own, padded), BF16),
        V((window, features), F32),
        V((2, R, features), BF16),
        V((2, R, features), BF16),
        V((nx, nz, ny, own, half), BF16),
        V((nx - 1, nz, ny, own, half), BF16),
        V((ny, nz, nx, own, half), BF16),
        V((ny - 1, nz, nx, own, half), BF16),
        V((ny - 1, nz, own, half), BF16),
        V((ny - 1, nz, own, half), BF16),
        V((nx - 1, nz, own, half), BF16),
        V((nx - 1, nz, own, half), BF16),
        V((nz, own, features), F32),
        V((nz, own, features), BF16),
        V((nz - 1, own, features), BF16),
        dma((12,)),
        dma((2,)),
        dma((2,)),
        dma,
        dma,
        dma((swaps,)),
        dma((swaps,)),
        dma((2,)),
        dma((2,)),
        dma((nx - 1,)),
        dma((nx - 1,)),
        dma((ny - 1,)),
        dma((ny - 1,)),
        dma((ny - 1,)),
        dma((ny - 1,)),
        dma((nx - 1,)),
        dma((nx - 1,)),
        dma((nz - 1,)),
        dma((nz - 1,)),
    ]
    updated, d_grid, d_wkv_t = pl.pallas_call(
        functools.partial(layer_kernel, sizes, factor),
        out_shape=(
            jax.ShapeDtypeStruct((nodes, features), BF16),
            jax.ShapeDtypeStruct((rows, features), BF16),
            jax.ShapeDtypeStruct((own, features), F32),
        ),
        in_specs=[hbm] * 9,
        out_specs=(hbm, hbm, hbm),
        scratch_shapes=scratch,
        compiler_params=pltpu.CompilerParams(
            collective_id=0, has_side_effects=True, vmem_limit_bytes=60 * 1024 * 1024
        ),
        name="encoder_layer",
    )(
        grid_latent[0],
        hidden[0],
        d_updated[0],
        w_kv,
        w_q,
        src_gain.reshape(1, features),
        q_gain.reshape(1, features),
        src_index.T,
        edge_mask.T,
    )
    updated, d_grid, d_wkv_t = pl.pallas_call(
        leave_kernel,
        out_shape=(
            jax.ShapeDtypeStruct((nodes, features), BF16),
            jax.ShapeDtypeStruct((rows, features), BF16),
            jax.ShapeDtypeStruct((own, features), F32),
        ),
        in_specs=[hbm, hbm, hbm],
        out_specs=(hbm, hbm, hbm),
        scratch_shapes=[
            V((nodes, features), BF16),
            V((rows, features), BF16),
            V((own, features), F32),
            dma((6,)),
        ],
        compiler_params=pltpu.CompilerParams(vmem_limit_bytes=60 * 1024 * 1024),
        name="leave",
    )(updated, d_grid, d_wkv_t)
    return (updated[None], d_grid[None], d_wkv_t)


def solution(mesh):
    bands, members = mesh.shape["band"], mesh.shape["ens"]
    nx = 4 if bands >= 64 else 2
    nz = bands // (2 * nx)
    finer = Mesh(mesh.devices.reshape(nz, nx, 2, members), AXES)
    cells = P("ens", BAND, None)
    in_specs = (cells, cells, cells, P(), P(), P(), P(), P(BAND, None), P(BAND, None))
    out_specs = (cells, cells, P(AXES, None))
    return jax.shard_map(
        functools.partial(per_device, (nz, nx, members)),
        mesh=finer,
        in_specs=in_specs,
        out_specs=out_specs,
        check_vma=False,
    )
```

```python
import functools
import math

import jax
import jax.numpy as jnp
from jax import lax
from jax.experimental import pallas as pl
from jax.experimental.pallas import tpu as pltpu
from jax.sharding import Mesh
from jax.sharding import PartitionSpec as P

HEADS = 16
K = 12
R = 32
BAND = ("bz", "bx", "bc")
AXES = ("bz", "bx", "bc", "ens")
EPSILON = 1e-05
MESH = pl.DeviceIdType.MESH
F32 = jnp.float32
BF16 = jnp.bfloat16
LANES = 128
WIDTHS = (256, 256)


def dot(left, right, contract):
    return lax.dot_general(left, right, ((contract[:1], contract[1:]), ((), ())), preferred_element_type=F32)


def normalize(values):
    average = jnp.mean(values, axis=-1, keepdims=True)
    centred = values - average
    variance = jnp.mean(centred * centred, axis=-1, keepdims=True)
    inv_std = lax.rsqrt(variance + EPSILON)
    return centred * inv_std, inv_std


def layer_kernel(
    sizes,
    factor,
    grid_hbm,
    hidden_hbm,
    cot_hbm,
    wkv_hbm,
    wq_hbm,
    src_gain_hbm,
    q_gain_hbm,
    index_hbm,
    mask_hbm,
    updated_hbm,
    dgrid_hbm,
    dw_hbm,
    updated_ref,
    dgrid_ref,
    dw_ref,
    out_sem,
    grid_ref,
    hidden_ref,
    cot_ref,
    src_gain_ref,
    q_gain_ref,
    index_ref,
    mask_ref,
    edge,
    wkv,
    wq,
    standard,
    inv_std,
    win,
    pair_win,
    kv,
    partial,
    parted,
    pair_parted,
    d_norm,
    back_send,
    back_recv,
    lots,
    load_sem,
    halo_send,
    halo_recv,
    win_send,
    win_recv,
    pair_send,
    pair_recv,
    back_ssem,
    back_rsem,
):
    nz, nx, ny = sizes
    nb = nz * nx * 2
    rows = grid_hbm.shape[0]
    nodes, features = hidden_hbm.shape
    window = rows + 2 * R
    half = features // 2
    own = dw_hbm.shape[0]

    z, x = lax.axis_index("bz"), lax.axis_index("bx")
    c, y = lax.axis_index("bc"), lax.axis_index("ens")
    band = (z * nx + x) * 2 + c

    def of_band(b):
        return (b // (2 * nx), (b // 2) % nx, b % 2, y)

    below = of_band((band + nb - 1) % nb)
    above = of_band((band + 1) % nb)
    pair = (z, x, 1 - c, y)

    def x_peer(k):
        return (z, (x + k) % nx, c, y)

    def y_peer(k):
        return (z, x, c, (y + k) % ny)

    def z_peer(k):
        return ((z + k) % nz, x, c, y)

    def remote(src, dst, ssem, rsem, device):
        return pltpu.make_async_remote_copy(
            src_ref=src, dst_ref=dst, send_sem=ssem, recv_sem=rsem, device_id=device, device_id_type=MESH
        )

    def load(src, dst, i):
        copy = pltpu.make_async_copy(src, dst, load_sem.at[i])
        copy.start()
        return copy

    load_grid = load(grid_hbm, grid_ref, 0)
    barrier = pltpu.get_barrier_semaphore()
    greeted = [below, above]
    greeted += [x_peer(k) for k in range(1, nx)]
    greeted += [y_peer(k) for k in range(1, ny)]
    greeted += [z_peer(k) for k in range(1, nz)]
    for device in greeted:
        pl.semaphore_signal(barrier, inc=1, device_id=device, device_id_type=MESH)

    load_gain = load(src_gain_hbm, src_gain_ref, 1)
    load_hidden = load(hidden_hbm, hidden_ref, 2)
    load_q_gain = load(q_gain_hbm, q_gain_ref, 3)
    load_index = load(index_hbm, index_ref, 5)
    load_mask = load(mask_hbm, mask_ref, 6)
    load_cot = load(cot_hbm, cot_ref, 7)
    load_q = load(wq_hbm, wq, 4)
    quarter = [slice(j * half, (j + 1) * half) for j in range(4)]
    load_kv = [load(wkv_hbm.at[:, cols], wkv.at[:, cols], 8 + j) for j, cols in enumerate(quarter)]

    load_grid.wait()
    pl.semaphore_wait(barrier, len(greeted))

    halo = [
        remote(grid_ref.at[0:R], edge.at[1], halo_send.at[0], halo_recv.at[0], below),
        remote(grid_ref.at[rows - R : rows], edge.at[0], halo_send.at[1], halo_recv.at[1], above),
    ]
    for copy in halo:
        copy.start()

    load_gain.wait()
    hat, scale = normalize(grid_ref[...].astype(F32))
    standard[...] = hat
    inv_std[...] = scale
    win[R : R + rows] = (hat * src_gain_ref[...]).astype(BF16)

    load_hidden.wait()
    load_q_gain.wait()
    hidden_hat, _ = normalize(hidden_ref[...].astype(F32))
    hidden_normed = (hidden_hat * q_gain_ref[...]).astype(BF16)
    load_q.wait()
    score_scale = 1.0 / math.sqrt(features // HEADS)
    queries = (dot(hidden_normed, wq[...], (1, 0)).astype(BF16).astype(F32) * score_scale).astype(BF16)

    load_index.wait()
    load_mask.wait()
    local = index_ref[...] - (band * rows - R)
    local = jnp.where(mask_ref[...] > 0, local, -1)
    row_ids = lax.broadcasted_iota(jnp.int32, (window, nodes), 0)
    times = jnp.zeros((window, nodes), F32)
    for j in range(K):
        times = times + jnp.where(local[j : j + 1, :] == row_ids, 1.0, 0.0)
    times = times.T
    times = jnp.concatenate([times, times], axis=0)
    live = times > 0.0

    for j, cols in enumerate(quarter):
        load_kv[j].wait()
        kv[R : R + rows, cols] = dot(win[R : R + rows], wkv[:, cols], (1, 0)).astype(BF16)
    for copy in halo:
        copy.wait_recv()
    hat, _ = normalize(edge[...].reshape(2 * R, features).astype(F32))
    outer = (hat * src_gain_ref[...]).astype(BF16)
    win[0:R] = outer[:R]
    win[R + rows : window] = outer[R:]
    swap_win = remote(win, pair_win, win_send, win_recv, pair)
    swap_win.start()
    for cols in quarter:
        tile = dot(outer, wkv[:, cols], (1, 0)).astype(BF16)
        kv[0:R, cols] = tile[:R]
        kv[R + rows : window, cols] = tile[R:]
    load_cot.wait()

    low_lane = lax.broadcasted_iota(jnp.int32, (nodes, LANES), 1) < features // HEADS
    cot = cot_ref[...]
    zero = jnp.zeros((nodes, LANES), F32)

    def two_heads(block):
        block = block.astype(F32)
        return jnp.concatenate(
            [jnp.where(low_lane, block, zero), jnp.where(low_lane, zero, block)], axis=0
        ).astype(BF16)

    group = ny * own

    swaps = []

    def keep_parted(first, tile):
        piece = min(LANES, group)
        for i in range(LANES // piece):
            at, inside = divmod(first + i * piece, group)
            parted[at % 2, at // (2 * nx), at // 2 % nx, inside : inside + piece, :window] = tile[i * piece : (i + 1) * piece]

    def swap(first, count):
        n = len(swaps)
        swaps.append(
            remote(
                parted.at[1 - c, first : first + count],
                pair_parted.at[first : first + count],
                pair_send.at[n],
                pair_recv.at[n],
                pair,
            )
        )
        swaps[-1].start()

    batches = 2 if nz >= 4 else 1
    blocks = features // LANES
    planes = nz // (2 * batches)
    for j in range(blocks):
        span = slice(j * LANES, (j + 1) * LANES)
        vspan = slice(features + j * LANES, features + (j + 1) * LANES)
        q2 = two_heads(queries[:, span])
        d2 = two_heads(cot[:, span])
        k_rows, v_rows = kv[:, span], kv[:, vspan]
        scores = dot(q2, k_rows, (1, 1))
        d_probs = dot(d2, v_rows, (1, 1))
        shifted = jnp.where(live, scores, -jnp.inf)
        terms = jnp.exp(shifted - jnp.max(shifted, axis=1, keepdims=True))
        probs = terms / jnp.sum(times * terms, axis=1, keepdims=True)
        weights = (times * probs.astype(BF16).astype(F32)).astype(BF16)
        counted = times * probs
        d_scores = (counted * (d_probs - jnp.sum(counted * d_probs, axis=1, keepdims=True))).astype(BF16)
        mixed = dot(weights, v_rows, (1, 0))
        attended = jnp.where(low_lane, mixed[:nodes], mixed[nodes:])
        updated_ref[:, span] = (hidden_ref[:, span].astype(F32) + attended).astype(BF16)
        partial[:, span] = dot(d_scores, q2, (0, 0)).astype(BF16)
        partial[:, vspan] = dot(weights, d2, (0, 0)).astype(BF16)
        keep_parted(j * LANES, dot(q2, d_scores, (0, 0)).astype(BF16))
        keep_parted(features + j * LANES, dot(d2, weights, (0, 0)).astype(BF16))
        if (j + 1) % (blocks // batches) == 0:
            batch = j * batches // blocks
            swap(batch * planes, planes)
            swap(nz // 2 + batch * planes, planes)

    outs = [pltpu.make_async_copy(updated_ref, updated_hbm, out_sem.at[0])]
    outs[0].start()
    swap_win.wait()
    for copy in swaps:
        copy.wait()

    def product(xd, cols):
        mine = jnp.concatenate([parted[c, i, xd, :, :window] for i in range(nz)], axis=0)
        other = jnp.concatenate([pair_parted[i, xd, :, :window] for i in range(nz)], axis=0)
        return dot(mine, win[:, cols], (1, 0)) + dot(other, pair_win[:, cols], (1, 0))

    starts = []
    left = 0
    for lot in lots:
        starts.append(left)
        left += lot["kept_a"].shape[-1]
    low, high = slice(0, nz // 2), slice(nz // 2, nz)

    def neighbours(lot, name, peer, piece):
        held, ssem, rsem = lot["recv_" + name], lot["ssem_" + name], lot["rsem_" + name]

        def forward(lot):
            over = lot["over_" + name]
            copies = [
                remote(piece(2).at[low], over.at[0], ssem.at[0], rsem.at[0], peer(1)),
                remote(piece(2).at[high], over.at[1], ssem.at[1], rsem.at[1], peer(3)),
            ]
            for copy in copies:
                copy.start()
            return copies

        def direct(k):
            i, part = (0, high) if k == 1 else (1, low)
            copy = remote(piece(k).at[part], held.at[i, part], ssem.at[2 + i], rsem.at[2 + i], peer(k))
            copy.start()
            return [copy]

        def augment(lot, forwards):
            over, copies = lot["over_" + name], []
            for i, (k, part) in enumerate([(1, low), (3, high)]):
                forwards[i].wait()
                target = piece(k).at[part]
                target[...] = (target[...].astype(F32) + over[i].astype(F32)).astype(BF16)
                copies.append(remote(target, held.at[i, part], ssem.at[4 + i], rsem.at[4 + i], peer(k)))
                copies[-1].start()
            return copies

        return forward, direct, augment

    first, augments = [], []
    for lot, start in zip(lots, starts):
        width = lot["kept_a"].shape[-1]
        send_a, send_b = lot["send_a"], lot["send_b"]
        forward_a, direct_a, augment_a = neighbours(lot, "a", x_peer, lambda k, ref=send_a: ref.at[k])
        forward_b, direct_b, augment_b = neighbours(lot, "b", y_peer, lambda k, ref=send_b: ref.at[(y + k) % ny])

        def x_piece(k):
            tile = product((x + k) % nx, slice(start, start + width))
            send_a[k] = tile.reshape(nz, ny, own, width).astype(BF16)

        x_piece(2)
        over_a = forward_a(lot)
        for xd in range(nx):
            tile = product(xd, slice(half + start, half + start + width))
            tile = tile.reshape(nz, ny, own, width).astype(BF16)
            for yd in range(ny):
                send_b[yd, :, xd] = tile[:, yd]
        over_b = forward_b(lot)
        copies_b = direct_b(1) + direct_b(3)
        x_piece(1)
        copies_a = direct_a(1)
        x_piece(3)
        copies_a += direct_a(3)
        x_piece(0)
        first.append((copies_a, copies_b))
        augments.append((augment_a, augment_b, over_a, over_b))

    part = partial[...]
    for j in range(2):
        cols = pl.ds(j * half, half)
        d_norm[:, cols] = dot(part, wkv[cols, :], (1, 1))
    back_send[0] = d_norm[0:R].astype(BF16)
    back_send[1] = d_norm[R + rows : window].astype(BF16)
    back = [
        remote(back_send.at[0], back_recv.at[0], back_ssem.at[0], back_rsem.at[0], below),
        remote(back_send.at[1], back_recv.at[1], back_ssem.at[1], back_rsem.at[1], above),
    ]
    for copy in back:
        copy.start()
    def second_exchange(lot, copies_a, copies_b):
        sent_a, sent_b = [], []
        for copy in copies_b:
            copy.wait()
        for k in list(range(1, nx)) + [0]:
            xd = (x + k) % nx
            total = lot["send_b"][y, :, xd].astype(F32)
            for j in range(2):
                total = total + lot["recv_b"][j, :, xd].astype(F32)
            if k:
                i = k - 1
                lot["send_b2"][i] = total.astype(BF16)
                src, dst = lot["send_b2"].at[i], lot["recv_b2"].at[i]
                sent_b.append(remote(src, dst, lot["b2_ssem"].at[i], lot["b2_rsem"].at[i], x_peer(k)))
                sent_b[-1].start()
            else:
                lot["kept_b"][...] = total
        for copy in copies_a:
            copy.wait()
        for k in list(range(1, ny)) + [0]:
            yd = (y + k) % ny
            total = lot["send_a"][0, :, yd].astype(F32)
            for j in range(2):
                total = total + lot["recv_a"][j, :, yd].astype(F32)
            if k:
                i = k - 1
                lot["send_a2"][i] = total.astype(BF16)
                src, dst = lot["send_a2"].at[i], lot["recv_a2"].at[i]
                sent_a.append(remote(src, dst, lot["a2_ssem"].at[i], lot["a2_rsem"].at[i], y_peer(k)))
                sent_a[-1].start()
            else:
                lot["kept_a"][...] = total
        return sent_a, sent_b

    def third_exchange(lot, copies_a, copies_b):
        width = lot["kept_a"].shape[-1]
        send, sent = lot["send_z"], []
        for copy in copies_b:
            copy.wait()
        total = lot["kept_b"][...]
        for j in range(nx - 1):
            total = total + lot["recv_b2"][j].astype(F32)
        send[:, :, width:] = total.astype(BF16)
        for copy in copies_a:
            copy.wait()
        total = lot["kept_a"][...]
        for j in range(ny - 1):
            total = total + lot["recv_a2"][j].astype(F32)
        send[:, :, :width] = total.astype(BF16)
        for k in range(1, nz):
            i, src = k - 1, send.at[(z + k) % nz]
            sent.append(remote(src, lot["recv_z"].at[i], lot["z_ssem"].at[i], lot["z_rsem"].at[i], z_peer(k)))
            sent[-1].start()
        return sent

    for lot, (augment_a, augment_b, over_a, over_b), (copies_a, copies_b) in zip(lots, augments, first):
        copies_a += augment_a(lot, over_a)
        copies_b += augment_b(lot, over_b)

    second = [second_exchange(lots[0], *first[0])]

    for copy in back:
        copy.wait()
    d_norm[R : 2 * R] += back_recv[1].astype(F32)
    d_norm[rows : rows + R] += back_recv[0].astype(F32)
    dx = d_norm[R : R + rows] * src_gain_ref[...]
    hat = standard[...]
    dgrid_ref[...] = (
        inv_std[...]
        * (dx - jnp.mean(dx, axis=-1, keepdims=True) - hat * jnp.mean(dx * hat, axis=-1, keepdims=True))
    ).astype(BF16)

    outs.append(pltpu.make_async_copy(dgrid_ref, dgrid_hbm, out_sem.at[1]))
    outs[1].start()

    for lot, copies in zip(lots[1:], first[1:]):
        second.append(second_exchange(lot, *copies))
    third = [third_exchange(lot, *copies) for lot, copies in zip(lots, second)]
    for lot, start, copies in zip(lots, starts, third):
        width = lot["kept_a"].shape[-1]
        total = lot["send_z"][z].astype(F32)
        for k in range(1, nz):
            copies[k - 1].wait()
            total = total + lot["recv_z"][k - 1].astype(F32)
        total = total * factor
        dw_ref[:, start : start + width] = total[:, :width]
        dw_ref[:, half + start : half + start + width] = total[:, width:]
    outs.append(pltpu.make_async_copy(dw_ref, dw_hbm, out_sem.at[2]))
    outs[2].start()
    for copy in outs:
        copy.wait()
    for copy in halo:
        copy.wait_send()


def leave_kernel(a, b, c, a_out, b_out, c_out, a_held, b_held, c_held, sem):
    into = [
        pltpu.make_async_copy(src, dst, sem.at[i]) for i, (src, dst) in enumerate([(b, b_held), (a, a_held), (c, c_held)])
    ]
    out = [
        pltpu.make_async_copy(src, dst, sem.at[3 + i])
        for i, (src, dst) in enumerate([(b_held, b_out), (a_held, a_out), (c_held, c_out)])
    ]
    for copy in into:
        copy.start()
    for first, second in zip(into, out):
        first.wait()
        second.start()
    for copy in out:
        copy.wait()


def per_device(sizes, grid_latent, hidden, d_updated, w_kv, w_q, src_gain, q_gain, src_index, edge_mask):
    nz, nx, ny = sizes
    _, rows, features = grid_latent.shape
    nodes = hidden.shape[1]
    window = rows + 2 * R
    half = features // 2
    columns = w_kv.shape[1]
    own = columns // (nz * nx * 2 * ny)
    factor = 1.0 / math.sqrt(ny * rows * nz * nx * 2)
    vmem = pl.BlockSpec(memory_space=pltpu.VMEM)
    hbm = pl.BlockSpec(memory_space=pltpu.HBM)
    dma = pltpu.SemaphoreType.DMA
    V = pltpu.VMEM
    padded = -(-window // LANES) * LANES
    swaps = 4 if nz >= 4 else 2
    lots = []
    for width in WIDTHS:
        lots.append(
            dict(
                send_a=V((nx, nz, ny, own, width), BF16),
                recv_a=V((2, nz, ny, own, width), BF16),
                over_a=V((2, nz // 2, ny, own, width), BF16),
                send_b=V((ny, nz, nx, own, width), BF16),
                recv_b=V((2, nz, nx, own, width), BF16),
                over_b=V((2, nz // 2, nx, own, width), BF16),
                send_a2=V((ny - 1, nz, own, width), BF16),
                recv_a2=V((ny - 1, nz, own, width), BF16),
                send_b2=V((nx - 1, nz, own, width), BF16),
                recv_b2=V((nx - 1, nz, own, width), BF16),
                kept_a=V((nz, own, width), F32),
                kept_b=V((nz, own, width), F32),
                send_z=V((nz, own, 2 * width), BF16),
                recv_z=V((nz - 1, own, 2 * width), BF16),
                ssem_a=dma((6,)),
                rsem_a=dma((6,)),
                ssem_b=dma((6,)),
                rsem_b=dma((6,)),
                a2_ssem=dma((ny - 1,)),
                a2_rsem=dma((ny - 1,)),
                b2_ssem=dma((nx - 1,)),
                b2_rsem=dma((nx - 1,)),
                z_ssem=dma((nz - 1,)),
                z_rsem=dma((nz - 1,)),
            )
        )
    scratch = [
        V((nodes, features), BF16),
        V((rows, features), BF16),
        V((own, features), F32),
        dma((3,)),
        V((rows, features), BF16),
        V((nodes, features), BF16),
        V((nodes, features), BF16),
        V((1, features), F32),
        V((1, features), F32),
        V((K, nodes), jnp.int32),
        V((K, nodes), jnp.int32),
        V((2, R, features), BF16),
        V((features, columns), BF16),
        V((features, features), BF16),
        V((rows, features), F32),
        V((rows, 1), F32),
        V((window, features), BF16),
        V((window, features), BF16),
        V((window, columns), BF16),
        V((window, columns), BF16),
        V((2, nz, nx, ny * own, padded), BF16),
        V((nz, nx, ny * own, padded), BF16),
        V((window, features), F32),
        V((2, R, features), BF16),
        V((2, R, features), BF16),
        lots,
        dma((12,)),
        dma((2,)),
        dma((2,)),
        dma,
        dma,
        dma((swaps,)),
        dma((swaps,)),
        dma((2,)),
        dma((2,)),
    ]
    updated, d_grid, d_wkv_t = pl.pallas_call(
        functools.partial(layer_kernel, sizes, factor),
        out_shape=(
            jax.ShapeDtypeStruct((nodes, features), BF16),
            jax.ShapeDtypeStruct((rows, features), BF16),
            jax.ShapeDtypeStruct((own, features), F32),
        ),
        in_specs=[hbm] * 9,
        out_specs=(hbm, hbm, hbm),
        scratch_shapes=scratch,
        compiler_params=pltpu.CompilerParams(
            collective_id=0, has_side_effects=True, vmem_limit_bytes=60 * 1024 * 1024
        ),
        name="encoder_layer",
    )(
        grid_latent[0],
        hidden[0],
        d_updated[0],
        w_kv,
        w_q,
        src_gain.reshape(1, features),
        q_gain.reshape(1, features),
        src_index.T,
        edge_mask.T,
    )
    updated, d_grid, d_wkv_t = pl.pallas_call(
        leave_kernel,
        out_shape=(
            jax.ShapeDtypeStruct((nodes, features), BF16),
            jax.ShapeDtypeStruct((rows, features), BF16),
            jax.ShapeDtypeStruct((own, features), F32),
        ),
        in_specs=[hbm, hbm, hbm],
        out_specs=(hbm, hbm, hbm),
        scratch_shapes=[
            V((nodes, features), BF16),
            V((rows, features), BF16),
            V((own, features), F32),
            dma((6,)),
        ],
        compiler_params=pltpu.CompilerParams(vmem_limit_bytes=60 * 1024 * 1024),
        name="leave",
    )(updated, d_grid, d_wkv_t)
    return (updated[None], d_grid[None], d_wkv_t)


def solution(mesh):
    bands, members = mesh.shape["band"], mesh.shape["ens"]
    nx = 4
    nz = bands // (2 * nx)
    finer = Mesh(mesh.devices.reshape(nz, nx, 2, members), AXES)
    cells = P("ens", BAND, None)
    in_specs = (cells, cells, cells, P(), P(), P(), P(), P(BAND, None), P(BAND, None))
    out_specs = (cells, cells, P(AXES, None))
    return jax.shard_map(
        functools.partial(per_device, (nz, nx, members)),
        mesh=finer,
        in_specs=in_specs,
        out_specs=out_specs,
        check_vma=False,
    )
```

```python
import functools
import math

import jax
import jax.numpy as jnp
from jax import lax
from jax.experimental import pallas as pl
from jax.experimental.pallas import tpu as pltpu
from jax.sharding import Mesh
from jax.sharding import PartitionSpec as P

HEADS = 16
K = 12
R = 32
BAND = ("bz", "bx", "bc")
AXES = ("bz", "bx", "bc", "ens")
EPSILON = 1e-05
MESH = pl.DeviceIdType.MESH
F32 = jnp.float32
BF16 = jnp.bfloat16
LANES = 128
WIDTHS = (256, 256)


def dot(left, right, contract):
    return lax.dot_general(left, right, ((contract[:1], contract[1:]), ((), ())), preferred_element_type=F32)


def normalize(values):
    average = jnp.mean(values, axis=-1, keepdims=True)
    centred = values - average
    variance = jnp.mean(centred * centred, axis=-1, keepdims=True)
    inv_std = lax.rsqrt(variance + EPSILON)
    return centred * inv_std, inv_std


def layer_kernel(
    sizes,
    factor,
    grid_hbm,
    hidden_hbm,
    cot_hbm,
    wkv_hbm,
    wq_hbm,
    src_gain_hbm,
    q_gain_hbm,
    index_hbm,
    mask_hbm,
    updated_hbm,
    dgrid_hbm,
    dw_hbm,
    updated_ref,
    dgrid_ref,
    dw_ref,
    out_sem,
    grid_ref,
    hidden_ref,
    cot_ref,
    src_gain_ref,
    q_gain_ref,
    index_ref,
    mask_ref,
    edge,
    wkv,
    wq,
    standard,
    inv_std,
    win,
    pair_win,
    kv,
    partial,
    parted,
    pair_parted,
    d_norm,
    back_send,
    back_recv,
    lots,
    load_sem,
    halo_send,
    halo_recv,
    win_send,
    win_recv,
    pair_send,
    pair_recv,
    back_ssem,
    back_rsem,
):
    nz, nx, ny = sizes
    nb = nz * nx * 2
    rows = grid_hbm.shape[0]
    nodes, features = hidden_hbm.shape
    window = rows + 2 * R
    half = features // 2
    own = dw_hbm.shape[0]

    z, x = lax.axis_index("bz"), lax.axis_index("bx")
    c, y = lax.axis_index("bc"), lax.axis_index("ens")
    band = (z * nx + x) * 2 + c

    def of_band(b):
        return (b // (2 * nx), (b // 2) % nx, b % 2, y)

    below = of_band((band + nb - 1) % nb)
    above = of_band((band + 1) % nb)
    pair = (z, x, 1 - c, y)

    def x_peer(k):
        return (z, (x + k) % nx, c, y)

    def y_peer(k):
        return (z, x, c, (y + k) % ny)

    def z_peer(k):
        return ((z + k) % nz, x, c, y)

    def remote(src, dst, ssem, rsem, device):
        return pltpu.make_async_remote_copy(
            src_ref=src, dst_ref=dst, send_sem=ssem, recv_sem=rsem, device_id=device, device_id_type=MESH
        )

    def load(src, dst, i):
        copy = pltpu.make_async_copy(src, dst, load_sem.at[i])
        copy.start()
        return copy

    load_grid = load(grid_hbm, grid_ref, 0)
    barrier = pltpu.get_barrier_semaphore()
    greeted = [below, above]
    greeted += [x_peer(k) for k in range(1, nx)]
    greeted += [y_peer(k) for k in range(1, ny)]
    greeted += [z_peer(k) for k in range(1, nz)]
    for device in greeted:
        pl.semaphore_signal(barrier, inc=1, device_id=device, device_id_type=MESH)

    load_gain = load(src_gain_hbm, src_gain_ref, 1)
    load_hidden = load(hidden_hbm, hidden_ref, 2)
    load_q_gain = load(q_gain_hbm, q_gain_ref, 3)
    load_index = load(index_hbm, index_ref, 5)
    load_mask = load(mask_hbm, mask_ref, 6)
    load_cot = load(cot_hbm, cot_ref, 7)
    load_q = load(wq_hbm, wq, 4)
    quarter = [slice(j * half, (j + 1) * half) for j in range(4)]
    load_kv = [load(wkv_hbm.at[:, cols], wkv.at[:, cols], 8 + j) for j, cols in enumerate(quarter)]

    load_grid.wait()
    pl.semaphore_wait(barrier, len(greeted))

    halo = [
        remote(grid_ref.at[0:R], edge.at[1], halo_send.at[0], halo_recv.at[0], below),
        remote(grid_ref.at[rows - R : rows], edge.at[0], halo_send.at[1], halo_recv.at[1], above),
    ]
    for copy in halo:
        copy.start()

    load_gain.wait()
    hat, scale = normalize(grid_ref[...].astype(F32))
    standard[...] = hat
    inv_std[...] = scale
    win[R : R + rows] = (hat * src_gain_ref[...]).astype(BF16)

    load_hidden.wait()
    load_q_gain.wait()
    hidden_hat, _ = normalize(hidden_ref[...].astype(F32))
    hidden_normed = (hidden_hat * q_gain_ref[...]).astype(BF16)
    load_q.wait()
    score_scale = 1.0 / math.sqrt(features // HEADS)
    queries = (dot(hidden_normed, wq[...], (1, 0)).astype(BF16).astype(F32) * score_scale).astype(BF16)

    load_index.wait()
    load_mask.wait()
    local = index_ref[...] - (band * rows - R)
    local = jnp.where(mask_ref[...] > 0, local, -1)
    row_ids = lax.broadcasted_iota(jnp.int32, (window, nodes), 0)
    times = jnp.zeros((window, nodes), F32)
    for j in range(K):
        times = times + jnp.where(local[j : j + 1, :] == row_ids, 1.0, 0.0)
    times = times.T
    times = jnp.concatenate([times, times], axis=0)
    live = times > 0.0

    for j, cols in enumerate(quarter):
        load_kv[j].wait()
        kv[R : R + rows, cols] = dot(win[R : R + rows], wkv[:, cols], (1, 0)).astype(BF16)
    for copy in halo:
        copy.wait_recv()
    hat, _ = normalize(edge[...].reshape(2 * R, features).astype(F32))
    outer = (hat * src_gain_ref[...]).astype(BF16)
    win[0:R] = outer[:R]
    win[R + rows : window] = outer[R:]
    swap_win = remote(win, pair_win, win_send, win_recv, pair)
    swap_win.start()
    for cols in quarter:
        tile = dot(outer, wkv[:, cols], (1, 0)).astype(BF16)
        kv[0:R, cols] = tile[:R]
        kv[R + rows : window, cols] = tile[R:]
    load_cot.wait()

    low_lane = lax.broadcasted_iota(jnp.int32, (nodes, LANES), 1) < features // HEADS
    cot = cot_ref[...]
    zero = jnp.zeros((nodes, LANES), F32)

    def two_heads(block):
        block = block.astype(F32)
        return jnp.concatenate(
            [jnp.where(low_lane, block, zero), jnp.where(low_lane, zero, block)], axis=0
        ).astype(BF16)

    group = ny * own

    swaps = []

    def keep_parted(first, tile):
        piece = min(LANES, group)
        for i in range(LANES // piece):
            at, inside = divmod(first + i * piece, group)
            parted[at % 2, at // (2 * nx), at // 2 % nx, inside : inside + piece, :window] = tile[i * piece : (i + 1) * piece]

    def swap(first, count):
        n = len(swaps)
        swaps.append(
            remote(
                parted.at[1 - c, first : first + count],
                pair_parted.at[first : first + count],
                pair_send.at[n],
                pair_recv.at[n],
                pair,
            )
        )
        swaps[-1].start()

    batches = 2 if nz >= 4 else 1
    blocks = features // LANES
    planes = nz // (2 * batches)
    def spans(j):
        return slice(j * LANES, (j + 1) * LANES), slice(features + j * LANES, features + (j + 1) * LANES)

    for batch in range(batches):
        mine = range(batch * blocks // batches, (batch + 1) * blocks // batches)
        q2s = [two_heads(queries[:, spans(j)[0]]) for j in mine]
        d2s = [two_heads(cot[:, spans(j)[0]]) for j in mine]
        scores = [dot(q2, kv[:, spans(j)[0]], (1, 1)) for q2, j in zip(q2s, mine)]
        d_probs = [dot(d2, kv[:, spans(j)[1]], (1, 1)) for d2, j in zip(d2s, mine)]
        weights, d_scores = [], []
        for score, d_prob in zip(scores, d_probs):
            shifted = jnp.where(live, score, -jnp.inf)
            terms = jnp.exp(shifted - jnp.max(shifted, axis=1, keepdims=True))
            probs = terms / jnp.sum(times * terms, axis=1, keepdims=True)
            weights.append((times * probs.astype(BF16).astype(F32)).astype(BF16))
            counted = times * probs
            d_scores.append((counted * (d_prob - jnp.sum(counted * d_prob, axis=1, keepdims=True))).astype(BF16))
        for j, q2, d2, weight, d_score in zip(mine, q2s, d2s, weights, d_scores):
            keep_parted(j * LANES, dot(q2, d_score, (0, 0)).astype(BF16))
            keep_parted(features + j * LANES, dot(d2, weight, (0, 0)).astype(BF16))
        swap(batch * planes, planes)
        swap(nz // 2 + batch * planes, planes)
        for j, q2, d2, weight, d_score in zip(mine, q2s, d2s, weights, d_scores):
            span, vspan = spans(j)
            mixed = dot(weight, kv[:, vspan], (1, 0))
            attended = jnp.where(low_lane, mixed[:nodes], mixed[nodes:])
            updated_ref[:, span] = (hidden_ref[:, span].astype(F32) + attended).astype(BF16)
            partial[:, span] = dot(d_score, q2, (0, 0)).astype(BF16)
            partial[:, vspan] = dot(weight, d2, (0, 0)).astype(BF16)

    outs = [pltpu.make_async_copy(updated_ref, updated_hbm, out_sem.at[0])]
    outs[0].start()
    swap_win.wait()
    for copy in swaps:
        copy.wait()

    def product(xd, cols):
        mine = jnp.concatenate([parted[c, i, xd, :, :window] for i in range(nz)], axis=0)
        other = jnp.concatenate([pair_parted[i, xd, :, :window] for i in range(nz)], axis=0)
        return dot(mine, win[:, cols], (1, 0)) + dot(other, pair_win[:, cols], (1, 0))

    starts = []
    left = 0
    for lot in lots:
        starts.append(left)
        left += lot["kept_a"].shape[-1]
    low, high = slice(0, nz // 2), slice(nz // 2, nz)

    def neighbours(lot, name, peer, piece):
        held, ssem, rsem = lot["recv_" + name], lot["ssem_" + name], lot["rsem_" + name]

        def forward(lot):
            over = lot["over_" + name]
            copies = [
                remote(piece(2).at[low], over.at[0], ssem.at[0], rsem.at[0], peer(1)),
                remote(piece(2).at[high], over.at[1], ssem.at[1], rsem.at[1], peer(3)),
            ]
            for copy in copies:
                copy.start()
            return copies

        def direct(k):
            i, part = (0, high) if k == 1 else (1, low)
            copy = remote(piece(k).at[part], held.at[i, part], ssem.at[2 + i], rsem.at[2 + i], peer(k))
            copy.start()
            return [copy]

        def augment(lot, forwards):
            over, copies = lot["over_" + name], []
            for i, (k, part) in enumerate([(1, low), (3, high)]):
                forwards[i].wait()
                target = piece(k).at[part]
                target[...] = (target[...].astype(F32) + over[i].astype(F32)).astype(BF16)
                copies.append(remote(target, held.at[i, part], ssem.at[4 + i], rsem.at[4 + i], peer(k)))
                copies[-1].start()
            return copies

        return forward, direct, augment

    first, augments = [], []
    for lot, start in zip(lots, starts):
        width = lot["kept_a"].shape[-1]
        send_a, send_b = lot["send_a"], lot["send_b"]
        forward_a, direct_a, augment_a = neighbours(lot, "a", x_peer, lambda k, ref=send_a: ref.at[k])
        forward_b, direct_b, augment_b = neighbours(lot, "b", y_peer, lambda k, ref=send_b: ref.at[(y + k) % ny])

        def x_piece(k):
            tile = product((x + k) % nx, slice(start, start + width))
            send_a[k] = tile.reshape(nz, ny, own, width).astype(BF16)

        x_piece(2)
        over_a = forward_a(lot)
        for xd in range(nx):
            tile = product(xd, slice(half + start, half + start + width))
            tile = tile.reshape(nz, ny, own, width).astype(BF16)
            for yd in range(ny):
                send_b[yd, :, xd] = tile[:, yd]
        over_b = forward_b(lot)
        copies_b = direct_b(1) + direct_b(3)
        x_piece(1)
        copies_a = direct_a(1)
        x_piece(3)
        copies_a += direct_a(3)
        x_piece(0)
        first.append((copies_a, copies_b))
        augments.append((augment_a, augment_b, over_a, over_b))

    def second_exchange(lot, copies_a, copies_b):
        sent_a, sent_b = [], []
        for copy in copies_b:
            copy.wait()
        for k in list(range(1, nx)) + [0]:
            xd = (x + k) % nx
            total = lot["send_b"][y, :, xd].astype(F32)
            for j in range(2):
                total = total + lot["recv_b"][j, :, xd].astype(F32)
            if k:
                i = k - 1
                lot["send_b2"][i] = total.astype(BF16)
                src, dst = lot["send_b2"].at[i], lot["recv_b2"].at[i]
                sent_b.append(remote(src, dst, lot["b2_ssem"].at[i], lot["b2_rsem"].at[i], x_peer(k)))
                sent_b[-1].start()
            else:
                lot["kept_b"][...] = total
        for copy in copies_a:
            copy.wait()
        for k in list(range(1, ny)) + [0]:
            yd = (y + k) % ny
            total = lot["send_a"][0, :, yd].astype(F32)
            for j in range(2):
                total = total + lot["recv_a"][j, :, yd].astype(F32)
            if k:
                i = k - 1
                lot["send_a2"][i] = total.astype(BF16)
                src, dst = lot["send_a2"].at[i], lot["recv_a2"].at[i]
                sent_a.append(remote(src, dst, lot["a2_ssem"].at[i], lot["a2_rsem"].at[i], y_peer(k)))
                sent_a[-1].start()
            else:
                lot["kept_a"][...] = total
        return sent_a, sent_b

    def third_exchange(lot, copies_a, copies_b):
        width = lot["kept_a"].shape[-1]
        send, sent = lot["send_z"], []
        for copy in copies_b:
            copy.wait()
        total = lot["kept_b"][...]
        for j in range(nx - 1):
            total = total + lot["recv_b2"][j].astype(F32)
        send[:, :, width:] = total.astype(BF16)
        for copy in copies_a:
            copy.wait()
        total = lot["kept_a"][...]
        for j in range(ny - 1):
            total = total + lot["recv_a2"][j].astype(F32)
        send[:, :, :width] = total.astype(BF16)
        for k in range(1, nz):
            i, src = k - 1, send.at[(z + k) % nz]
            sent.append(remote(src, lot["recv_z"].at[i], lot["z_ssem"].at[i], lot["z_rsem"].at[i], z_peer(k)))
            sent[-1].start()
        return sent

    for lot, (augment_a, augment_b, over_a, over_b), (copies_a, copies_b) in zip(lots, augments, first):
        copies_a += augment_a(lot, over_a)
        copies_b += augment_b(lot, over_b)

    part = partial[...]
    for j in range(2):
        cols = pl.ds(j * half, half)
        d_norm[:, cols] = dot(part, wkv[cols, :], (1, 1))
    back_send[0] = d_norm[0:R].astype(BF16)
    back_send[1] = d_norm[R + rows : window].astype(BF16)
    back = [
        remote(back_send.at[0], back_recv.at[0], back_ssem.at[0], back_rsem.at[0], below),
        remote(back_send.at[1], back_recv.at[1], back_ssem.at[1], back_rsem.at[1], above),
    ]
    for copy in back:
        copy.start()
    second = [second_exchange(lots[0], *first[0])]

    for lot, copies in zip(lots[1:], first[1:]):
        second.append(second_exchange(lot, *copies))
    third = [third_exchange(lot, *copies) for lot, copies in zip(lots, second)]
    for copy in back:
        copy.wait()
    d_norm[R : 2 * R] += back_recv[1].astype(F32)
    d_norm[rows : rows + R] += back_recv[0].astype(F32)
    dx = d_norm[R : R + rows] * src_gain_ref[...]
    hat = standard[...]
    dgrid_ref[...] = (
        inv_std[...]
        * (dx - jnp.mean(dx, axis=-1, keepdims=True) - hat * jnp.mean(dx * hat, axis=-1, keepdims=True))
    ).astype(BF16)

    outs.append(pltpu.make_async_copy(dgrid_ref, dgrid_hbm, out_sem.at[1]))
    outs[1].start()

    for lot, start, copies in zip(lots, starts, third):
        width = lot["kept_a"].shape[-1]
        total = lot["send_z"][z].astype(F32)
        for k in range(1, nz):
            copies[k - 1].wait()
            total = total + lot["recv_z"][k - 1].astype(F32)
        total = total * factor
        dw_ref[:, start : start + width] = total[:, :width]
        dw_ref[:, half + start : half + start + width] = total[:, width:]
    outs.append(pltpu.make_async_copy(dw_ref, dw_hbm, out_sem.at[2]))
    outs[2].start()
    for copy in outs:
        copy.wait()
    for copy in halo:
        copy.wait_send()


def leave_kernel(a, b, c, a_out, b_out, c_out, a_held, b_held, c_held, sem):
    into = [
        pltpu.make_async_copy(src, dst, sem.at[i]) for i, (src, dst) in enumerate([(b, b_held), (a, a_held), (c, c_held)])
    ]
    out = [
        pltpu.make_async_copy(src, dst, sem.at[3 + i])
        for i, (src, dst) in enumerate([(b_held, b_out), (a_held, a_out), (c_held, c_out)])
    ]
    for copy in into:
        copy.start()
    for first, second in zip(into, out):
        first.wait()
        second.start()
    for copy in out:
        copy.wait()


def per_device(sizes, grid_latent, hidden, d_updated, w_kv, w_q, src_gain, q_gain, src_index, edge_mask):
    nz, nx, ny = sizes
    _, rows, features = grid_latent.shape
    nodes = hidden.shape[1]
    window = rows + 2 * R
    half = features // 2
    columns = w_kv.shape[1]
    own = columns // (nz * nx * 2 * ny)
    factor = 1.0 / math.sqrt(ny * rows * nz * nx * 2)
    vmem = pl.BlockSpec(memory_space=pltpu.VMEM)
    hbm = pl.BlockSpec(memory_space=pltpu.HBM)
    dma = pltpu.SemaphoreType.DMA
    V = pltpu.VMEM
    padded = -(-window // LANES) * LANES
    swaps = 4 if nz >= 4 else 2
    lots = []
    for width in WIDTHS:
        lots.append(
            dict(
                send_a=V((nx, nz, ny, own, width), BF16),
                recv_a=V((2, nz, ny, own, width), BF16),
                over_a=V((2, nz // 2, ny, own, width), BF16),
                send_b=V((ny, nz, nx, own, width), BF16),
                recv_b=V((2, nz, nx, own, width), BF16),
                over_b=V((2, nz // 2, nx, own, width), BF16),
                send_a2=V((ny - 1, nz, own, width), BF16),
                recv_a2=V((ny - 1, nz, own, width), BF16),
                send_b2=V((nx - 1, nz, own, width), BF16),
                recv_b2=V((nx - 1, nz, own, width), BF16),
                kept_a=V((nz, own, width), F32),
                kept_b=V((nz, own, width), F32),
                send_z=V((nz, own, 2 * width), BF16),
                recv_z=V((nz - 1, own, 2 * width), BF16),
                ssem_a=dma((6,)),
                rsem_a=dma((6,)),
                ssem_b=dma((6,)),
                rsem_b=dma((6,)),
                a2_ssem=dma((ny - 1,)),
                a2_rsem=dma((ny - 1,)),
                b2_ssem=dma((nx - 1,)),
                b2_rsem=dma((nx - 1,)),
                z_ssem=dma((nz - 1,)),
                z_rsem=dma((nz - 1,)),
            )
        )
    scratch = [
        V((nodes, features), BF16),
        V((rows, features), BF16),
        V((own, features), F32),
        dma((3,)),
        V((rows, features), BF16),
        V((nodes, features), BF16),
        V((nodes, features), BF16),
        V((1, features), F32),
        V((1, features), F32),
        V((K, nodes), jnp.int32),
        V((K, nodes), jnp.int32),
        V((2, R, features), BF16),
        V((features, columns), BF16),
        V((features, features), BF16),
        V((rows, features), F32),
        V((rows, 1), F32),
        V((window, features), BF16),
        V((window, features), BF16),
        V((window, columns), BF16),
        V((window, columns), BF16),
        V((2, nz, nx, ny * own, padded), BF16),
        V((nz, nx, ny * own, padded), BF16),
        V((window, features), F32),
        V((2, R, features), BF16),
        V((2, R, features), BF16),
        lots,
        dma((12,)),
        dma((2,)),
        dma((2,)),
        dma,
        dma,
        dma((swaps,)),
        dma((swaps,)),
        dma((2,)),
        dma((2,)),
    ]
    updated, d_grid, d_wkv_t = pl.pallas_call(
        functools.partial(layer_kernel, sizes, factor),
        out_shape=(
            jax.ShapeDtypeStruct((nodes, features), BF16),
            jax.ShapeDtypeStruct((rows, features), BF16),
            jax.ShapeDtypeStruct((own, features), F32),
        ),
        in_specs=[hbm] * 9,
        out_specs=(hbm, hbm, hbm),
        scratch_shapes=scratch,
        compiler_params=pltpu.CompilerParams(
            collective_id=0, has_side_effects=True, vmem_limit_bytes=60 * 1024 * 1024
        ),
        name="encoder_layer",
    )(
        grid_latent[0],
        hidden[0],
        d_updated[0],
        w_kv,
        w_q,
        src_gain.reshape(1, features),
        q_gain.reshape(1, features),
        src_index.T,
        edge_mask.T,
    )
    updated, d_grid, d_wkv_t = pl.pallas_call(
        leave_kernel,
        out_shape=(
            jax.ShapeDtypeStruct((nodes, features), BF16),
            jax.ShapeDtypeStruct((rows, features), BF16),
            jax.ShapeDtypeStruct((own, features), F32),
        ),
        in_specs=[hbm, hbm, hbm],
        out_specs=(hbm, hbm, hbm),
        scratch_shapes=[
            V((nodes, features), BF16),
            V((rows, features), BF16),
            V((own, features), F32),
            dma((6,)),
        ],
        compiler_params=pltpu.CompilerParams(vmem_limit_bytes=60 * 1024 * 1024),
        name="leave",
    )(updated, d_grid, d_wkv_t)
    return (updated[None], d_grid[None], d_wkv_t)


def solution(mesh):
    bands, members = mesh.shape["band"], mesh.shape["ens"]
    nx = 4
    nz = bands // (2 * nx)
    finer = Mesh(mesh.devices.reshape(nz, nx, 2, members), AXES)
    cells = P("ens", BAND, None)
    in_specs = (cells, cells, cells, P(), P(), P(), P(), P(BAND, None), P(BAND, None))
    out_specs = (cells, cells, P(AXES, None))
    return jax.shard_map(
        functools.partial(per_device, (nz, nx, members)),
        mesh=finer,
        in_specs=in_specs,
        out_specs=out_specs,
        check_vma=False,
    )
```

```python
import functools
import math

import jax
import jax.numpy as jnp
from jax import lax
from jax.experimental import pallas as pl
from jax.experimental.pallas import tpu as pltpu
from jax.sharding import Mesh
from jax.sharding import PartitionSpec as P

HEADS = 16
K = 12
R = 32
BAND = ("bz", "bx", "bc")
AXES = ("bz", "bx", "bc", "ens")
EPSILON = 1e-05
MESH = pl.DeviceIdType.MESH
F32 = jnp.float32
BF16 = jnp.bfloat16
LANES = 128
WIDTHS = (256, 128, 128)


def dot(left, right, contract):
    return lax.dot_general(left, right, ((contract[:1], contract[1:]), ((), ())), preferred_element_type=F32)


def normalize(values):
    average = jnp.mean(values, axis=-1, keepdims=True)
    centred = values - average
    variance = jnp.mean(centred * centred, axis=-1, keepdims=True)
    inv_std = lax.rsqrt(variance + EPSILON)
    return centred * inv_std, inv_std


def layer_kernel(
    sizes,
    factor,
    grid_hbm,
    hidden_hbm,
    cot_hbm,
    wkv_hbm,
    wq_hbm,
    src_gain_hbm,
    q_gain_hbm,
    index_hbm,
    mask_hbm,
    updated_ref,
    dgrid_ref,
    dw_ref,
    grid_ref,
    hidden_ref,
    cot_ref,
    src_gain_ref,
    q_gain_ref,
    index_ref,
    mask_ref,
    edge,
    pairs,
    inner,
    wkv,
    wq,
    standard,
    inv_std,
    win,
    pair_win,
    kv,
    partial,
    parted,
    pair_parted,
    d_norm,
    back_send,
    back_recv,
    lots,
    load_sem,
    halo_send,
    halo_recv,
    win_send,
    win_recv,
    pair_send,
    pair_recv,
    back_ssem,
    back_rsem,
):
    nz, nx, ny = sizes
    nb = nz * nx * 2
    rows = grid_hbm.shape[0]
    nodes, features = hidden_hbm.shape
    window = rows + 2 * R
    half = features // 2
    own = dw_ref.shape[0]

    z, x = lax.axis_index("bz"), lax.axis_index("bx")
    c, y = lax.axis_index("bc"), lax.axis_index("ens")
    band = (z * nx + x) * 2 + c

    def of_band(b):
        return (b // (2 * nx), (b // 2) % nx, b % 2, y)

    below = of_band((band + nb - 1) % nb)
    above = of_band((band + 1) % nb)
    pair = (z, x, 1 - c, y)

    def x_peer(k):
        return (z, (x + k) % nx, c, y)

    def y_peer(k):
        return (z, x, c, (y + k) % ny)

    def z_peer(k):
        return ((z + k) % nz, x, c, y)

    def remote(src, dst, ssem, rsem, device):
        return pltpu.make_async_remote_copy(
            src_ref=src, dst_ref=dst, send_sem=ssem, recv_sem=rsem, device_id=device, device_id_type=MESH
        )

    def load(src, dst, i):
        copy = pltpu.make_async_copy(src, dst, load_sem.at[i])
        copy.start()
        return copy

    load_grid = load(grid_hbm, grid_ref, 0)
    barrier = pltpu.get_barrier_semaphore()
    greeted = [below, above]
    greeted += [x_peer(k) for k in range(1, nx)]
    greeted += [y_peer(k) for k in range(1, ny)]
    greeted += [z_peer(k) for k in range(1, nz)]
    for device in greeted:
        pl.semaphore_signal(barrier, inc=1, device_id=device, device_id_type=MESH)

    load_gain = load(src_gain_hbm, src_gain_ref, 1)
    load_hidden = load(hidden_hbm, hidden_ref, 2)
    load_q_gain = load(q_gain_hbm, q_gain_ref, 3)
    load_index = load(index_hbm, index_ref, 5)
    load_mask = load(mask_hbm, mask_ref, 6)
    load_cot = load(cot_hbm, cot_ref, 7)
    load_q = load(wq_hbm, wq, 4)
    quarter = [slice(j * half, (j + 1) * half) for j in range(4)]
    load_kv = [load(wkv_hbm.at[:, cols], wkv.at[:, cols], 8 + j) for j, cols in enumerate(quarter)]

    load_grid.wait()
    pl.semaphore_wait(barrier, len(greeted))

    halo = [
        remote(grid_ref.at[0:R], edge.at[1], halo_send.at[0], halo_recv.at[0], below),
        remote(grid_ref.at[rows - R : rows], edge.at[0], halo_send.at[1], halo_recv.at[1], above),
    ]
    for copy in halo:
        copy.start()

    load_gain.wait()
    hat, scale = normalize(grid_ref[...].astype(F32))
    standard[...] = hat
    inv_std[...] = scale
    win[:rows] = (hat * src_gain_ref[...]).astype(BF16)

    load_hidden.wait()
    load_q_gain.wait()
    hidden_hat, _ = normalize(hidden_ref[...].astype(F32))
    hidden_normed = (hidden_hat * q_gain_ref[...]).astype(BF16)
    load_q.wait()
    score_scale = 1.0 / math.sqrt(features // HEADS)
    queries = (dot(hidden_normed, wq[...], (1, 0)).astype(BF16).astype(F32) * score_scale).astype(BF16)

    load_index.wait()
    load_mask.wait()
    local = index_ref[...] - (band * rows - R)
    local = jnp.where(mask_ref[...] > 0, local, -1)
    row_ids = lax.broadcasted_iota(jnp.int32, (window, nodes), 0)
    row_ids = jnp.where(row_ids < rows, row_ids + R, jnp.where(row_ids < rows + R, row_ids - rows, row_ids))
    times = jnp.zeros((window, nodes), F32)
    for j in range(K):
        times = times + jnp.where(local[j : j + 1, :] == row_ids, 1.0, 0.0)
    times = times.T
    times = jnp.concatenate([times, times], axis=0)
    live = times > 0.0

    for j, cols in enumerate(quarter):
        load_kv[j].wait()
        kv[:rows, cols] = dot(win[:rows], wkv[:, cols], (1, 0)).astype(BF16)
    load_cot.wait()
    low_lane = lax.broadcasted_iota(jnp.int32, (nodes, LANES), 1) < features // HEADS
    cot = cot_ref[...]
    zero = jnp.zeros((nodes, LANES), F32)

    def two_heads(block):
        block = block.astype(F32)
        return jnp.concatenate(
            [jnp.where(low_lane, block, zero), jnp.where(low_lane, zero, block)], axis=0
        ).astype(BF16)

    def spans(j):
        return slice(j * LANES, (j + 1) * LANES), slice(features + j * LANES, features + (j + 1) * LANES)

    for j in range(features // LANES):
        span, vspan = spans(j)
        q2 = two_heads(queries[:, span])
        d2 = two_heads(cot[:, span])
        pairs[0, j], pairs[1, j] = q2, d2
        inner[0, j] = dot(q2, kv[:rows, span], (1, 1))
        inner[1, j] = dot(d2, kv[:rows, vspan], (1, 1))

    for copy in halo:
        copy.wait_recv()
    hat, _ = normalize(edge[...].reshape(2 * R, features).astype(F32))
    outer = (hat * src_gain_ref[...]).astype(BF16)
    win[rows:] = outer
    swap_win = remote(win, pair_win, win_send, win_recv, pair)
    swap_win.start()
    for cols in quarter:
        kv[rows:, cols] = dot(outer, wkv[:, cols], (1, 0)).astype(BF16)
    group = ny * own

    swaps = []

    def keep_parted(first, tile):
        piece = min(LANES, group)
        for i in range(LANES // piece):
            at, inside = divmod(first + i * piece, group)
            parted[at % 2, at // (2 * nx), at // 2 % nx, inside : inside + piece, :window] = tile[i * piece : (i + 1) * piece]

    def swap(first, count):
        n = len(swaps)
        swaps.append(
            remote(
                parted.at[1 - c, first : first + count],
                pair_parted.at[first : first + count],
                pair_send.at[n],
                pair_recv.at[n],
                pair,
            )
        )
        swaps[-1].start()

    batches = 2 if nz >= 4 else 1
    blocks = features // LANES
    planes = nz // (2 * batches)
    for batch in range(batches):
        mine = range(batch * blocks // batches, (batch + 1) * blocks // batches)
        q2s = [pairs[0, j] for j in mine]
        d2s = [pairs[1, j] for j in mine]
        scores = [
            jnp.concatenate([inner[0, j], dot(q2, kv[rows:, spans(j)[0]], (1, 1))], axis=1) for q2, j in zip(q2s, mine)
        ]
        d_probs = [
            jnp.concatenate([inner[1, j], dot(d2, kv[rows:, spans(j)[1]], (1, 1))], axis=1) for d2, j in zip(d2s, mine)
        ]
        weights, d_scores = [], []
        for score, d_prob in zip(scores, d_probs):
            shifted = jnp.where(live, score, -jnp.inf)
            terms = jnp.exp(shifted - jnp.max(shifted, axis=1, keepdims=True))
            probs = terms / jnp.sum(times * terms, axis=1, keepdims=True)
            weights.append((times * probs.astype(BF16).astype(F32)).astype(BF16))
            counted = times * probs
            d_scores.append((counted * (d_prob - jnp.sum(counted * d_prob, axis=1, keepdims=True))).astype(BF16))
        for j, q2, d2, weight, d_score in zip(mine, q2s, d2s, weights, d_scores):
            keep_parted(j * LANES, dot(q2, d_score, (0, 0)).astype(BF16))
            keep_parted(features + j * LANES, dot(d2, weight, (0, 0)).astype(BF16))
        swap(batch * planes, planes)
        swap(nz // 2 + batch * planes, planes)
        for j, q2, d2, weight, d_score in zip(mine, q2s, d2s, weights, d_scores):
            span, vspan = spans(j)
            mixed = dot(weight, kv[:, vspan], (1, 0))
            attended = jnp.where(low_lane, mixed[:nodes], mixed[nodes:])
            updated_ref[:, span] = (hidden_ref[:, span].astype(F32) + attended).astype(BF16)
            partial[:, span] = dot(d_score, q2, (0, 0)).astype(BF16)
            partial[:, vspan] = dot(weight, d2, (0, 0)).astype(BF16)

    swap_win.wait()
    for copy in swaps:
        copy.wait()

    def product(xd, cols):
        mine = jnp.concatenate([parted[c, i, xd, :, :window] for i in range(nz)], axis=0)
        other = jnp.concatenate([pair_parted[i, xd, :, :window] for i in range(nz)], axis=0)
        return dot(mine, win[:, cols], (1, 0)) + dot(other, pair_win[:, cols], (1, 0))

    starts = []
    left = 0
    for lot in lots:
        starts.append(left)
        left += lot["kept_a"].shape[-1]
    low, high = slice(0, nz // 2), slice(nz // 2, nz)

    def neighbours(lot, name, peer, piece):
        held, ssem, rsem = lot["recv_" + name], lot["ssem_" + name], lot["rsem_" + name]

        def forward(lot):
            over = lot["over_" + name]
            copies = [
                remote(piece(2).at[low], over.at[0], ssem.at[0], rsem.at[0], peer(1)),
                remote(piece(2).at[high], over.at[1], ssem.at[1], rsem.at[1], peer(3)),
            ]
            for copy in copies:
                copy.start()
            return copies

        def direct(k):
            i, part = (0, high) if k == 1 else (1, low)
            copy = remote(piece(k).at[part], held.at[i, part], ssem.at[2 + i], rsem.at[2 + i], peer(k))
            copy.start()
            return [copy]

        def augment(lot, forwards):
            over, copies = lot["over_" + name], []
            for i, (k, part) in enumerate([(1, low), (3, high)]):
                forwards[i].wait()
                target = piece(k).at[part]
                target[...] = (target[...].astype(F32) + over[i].astype(F32)).astype(BF16)
                copies.append(remote(target, held.at[i, part], ssem.at[4 + i], rsem.at[4 + i], peer(k)))
                copies[-1].start()
            return copies

        return forward, direct, augment

    first, augments = [], []
    for lot, start in zip(lots, starts):
        width = lot["kept_a"].shape[-1]
        send_a, send_b = lot["send_a"], lot["send_b"]
        forward_a, direct_a, augment_a = neighbours(lot, "a", x_peer, lambda k, ref=send_a: ref.at[k])
        forward_b, direct_b, augment_b = neighbours(lot, "b", y_peer, lambda k, ref=send_b: ref.at[(y + k) % ny])

        def x_piece(k):
            tile = product((x + k) % nx, slice(start, start + width))
            send_a[k] = tile.reshape(nz, ny, own, width).astype(BF16)

        x_piece(2)
        over_a = forward_a(lot)
        for xd in range(nx):
            tile = product(xd, slice(half + start, half + start + width))
            tile = tile.reshape(nz, ny, own, width).astype(BF16)
            for yd in range(ny):
                send_b[yd, :, xd] = tile[:, yd]
        over_b = forward_b(lot)
        copies_b = direct_b(1) + direct_b(3)
        x_piece(1)
        copies_a = direct_a(1)
        x_piece(3)
        copies_a += direct_a(3)
        x_piece(0)
        first.append((copies_a, copies_b))
        augments.append((augment_a, augment_b, over_a, over_b))

    def second_exchange(lot, copies_a, copies_b):
        sent_a, sent_b = [], []
        for copy in copies_b:
            copy.wait()
        for k in list(range(1, nx)) + [0]:
            xd = (x + k) % nx
            total = lot["send_b"][y, :, xd].astype(F32)
            for j in range(2):
                total = total + lot["recv_b"][j, :, xd].astype(F32)
            if k:
                i = k - 1
                lot["send_b2"][i] = total.astype(BF16)
                src, dst = lot["send_b2"].at[i], lot["recv_b2"].at[i]
                sent_b.append(remote(src, dst, lot["b2_ssem"].at[i], lot["b2_rsem"].at[i], x_peer(k)))
                sent_b[-1].start()
            else:
                lot["kept_b"][...] = total
        for copy in copies_a:
            copy.wait()
        for k in list(range(1, ny)) + [0]:
            yd = (y + k) % ny
            total = lot["send_a"][0, :, yd].astype(F32)
            for j in range(2):
                total = total + lot["recv_a"][j, :, yd].astype(F32)
            if k:
                i = k - 1
                lot["send_a2"][i] = total.astype(BF16)
                src, dst = lot["send_a2"].at[i], lot["recv_a2"].at[i]
                sent_a.append(remote(src, dst, lot["a2_ssem"].at[i], lot["a2_rsem"].at[i], y_peer(k)))
                sent_a[-1].start()
            else:
                lot["kept_a"][...] = total
        return sent_a, sent_b

    def third_exchange(lot, copies_a, copies_b):
        width = lot["kept_a"].shape[-1]
        send, sent = lot["send_z"], []
        for copy in copies_b:
            copy.wait()
        total = lot["kept_b"][...]
        for j in range(nx - 1):
            total = total + lot["recv_b2"][j].astype(F32)
        send[:, :, width:] = total.astype(BF16)
        for copy in copies_a:
            copy.wait()
        total = lot["kept_a"][...]
        for j in range(ny - 1):
            total = total + lot["recv_a2"][j].astype(F32)
        send[:, :, :width] = total.astype(BF16)
        for k in sorted(range(1, nz), key=lambda k: abs(2 * k - nz)):
            i, src = k - 1, send.at[(z + k) % nz]
            sent.append(remote(src, lot["recv_z"].at[i], lot["z_ssem"].at[i], lot["z_rsem"].at[i], z_peer(k)))
            sent[-1].start()
        return sent

    for lot, (augment_a, augment_b, over_a, over_b), (copies_a, copies_b) in zip(lots, augments, first):
        copies_a += augment_a(lot, over_a)
        copies_b += augment_b(lot, over_b)

    part = partial[...]
    for j in range(2):
        cols = pl.ds(j * half, half)
        d_norm[:, cols] = dot(part, wkv[cols, :], (1, 1))
    back_send[0] = d_norm[rows : rows + R].astype(BF16)
    back_send[1] = d_norm[rows + R : window].astype(BF16)
    back = [
        remote(back_send.at[0], back_recv.at[0], back_ssem.at[0], back_rsem.at[0], below),
        remote(back_send.at[1], back_recv.at[1], back_ssem.at[1], back_rsem.at[1], above),
    ]
    for copy in back:
        copy.start()
    second = [second_exchange(lots[0], *first[0])]

    for lot, copies in zip(lots[1:], first[1:]):
        second.append(second_exchange(lot, *copies))
    third = [third_exchange(lot, *copies) for lot, copies in zip(lots, second)]
    for copy in back:
        copy.wait()
    d_norm[:R] += back_recv[1].astype(F32)
    d_norm[rows - R : rows] += back_recv[0].astype(F32)
    dx = d_norm[:rows] * src_gain_ref[...]
    hat = standard[...]
    dgrid_ref[...] = (
        inv_std[...]
        * (dx - jnp.mean(dx, axis=-1, keepdims=True) - hat * jnp.mean(dx * hat, axis=-1, keepdims=True))
    ).astype(BF16)


    for lot, start, copies in zip(lots, starts, third):
        width = lot["kept_a"].shape[-1]
        total = lot["send_z"][z].astype(F32)
        for copy in copies:
            copy.wait()
        for k in range(1, nz):
            total = total + lot["recv_z"][k - 1].astype(F32)
        total = total * factor
        dw_ref[:, start : start + width] = total[:, :width]
        dw_ref[:, half + start : half + start + width] = total[:, width:]
    for copy in halo:
        copy.wait_send()


def leave_kernel(a, b, c, a_out, b_out, c_out, sem):
    copies = [
        pltpu.make_async_copy(src, dst, sem.at[i])
        for i, (src, dst) in enumerate([(b, b_out), (a, a_out), (c, c_out)])
    ]
    for copy in copies:
        copy.start()
    for copy in copies:
        copy.wait()


def per_device(sizes, grid_latent, hidden, d_updated, w_kv, w_q, src_gain, q_gain, src_index, edge_mask):
    nz, nx, ny = sizes
    _, rows, features = grid_latent.shape
    nodes = hidden.shape[1]
    window = rows + 2 * R
    half = features // 2
    columns = w_kv.shape[1]
    own = columns // (nz * nx * 2 * ny)
    factor = 1.0 / math.sqrt(ny * rows * nz * nx * 2)
    vmem = pl.BlockSpec(memory_space=pltpu.VMEM)
    hbm = pl.BlockSpec(memory_space=pltpu.HBM)
    dma = pltpu.SemaphoreType.DMA
    V = pltpu.VMEM
    padded = -(-window // LANES) * LANES
    swaps = 4 if nz >= 4 else 2
    lots = []
    for width in WIDTHS:
        lots.append(
            dict(
                send_a=V((nx, nz, ny, own, width), BF16),
                recv_a=V((2, nz, ny, own, width), BF16),
                over_a=V((2, nz // 2, ny, own, width), BF16),
                send_b=V((ny, nz, nx, own, width), BF16),
                recv_b=V((2, nz, nx, own, width), BF16),
                over_b=V((2, nz // 2, nx, own, width), BF16),
                send_a2=V((ny - 1, nz, own, width), BF16),
                recv_a2=V((ny - 1, nz, own, width), BF16),
                send_b2=V((nx - 1, nz, own, width), BF16),
                recv_b2=V((nx - 1, nz, own, width), BF16),
                kept_a=V((nz, own, width), F32),
                kept_b=V((nz, own, width), F32),
                send_z=V((nz, own, 2 * width), BF16),
                recv_z=V((nz - 1, own, 2 * width), BF16),
                ssem_a=dma((6,)),
                rsem_a=dma((6,)),
                ssem_b=dma((6,)),
                rsem_b=dma((6,)),
                a2_ssem=dma((ny - 1,)),
                a2_rsem=dma((ny - 1,)),
                b2_ssem=dma((nx - 1,)),
                b2_rsem=dma((nx - 1,)),
                z_ssem=dma((nz - 1,)),
                z_rsem=dma((nz - 1,)),
            )
        )
    scratch = [
        V((rows, features), BF16),
        V((nodes, features), BF16),
        V((nodes, features), BF16),
        V((1, features), F32),
        V((1, features), F32),
        V((K, nodes), jnp.int32),
        V((K, nodes), jnp.int32),
        V((2, R, features), BF16),
        V((2, features // LANES, 2 * nodes, LANES), BF16),
        V((2, features // LANES, 2 * nodes, rows), F32),
        V((features, columns), BF16),
        V((features, features), BF16),
        V((rows, features), F32),
        V((rows, 1), F32),
        V((window, features), BF16),
        V((window, features), BF16),
        V((window, columns), BF16),
        V((window, columns), BF16),
        V((2, nz, nx, ny * own, padded), BF16),
        V((nz, nx, ny * own, padded), BF16),
        V((window, features), F32),
        V((2, R, features), BF16),
        V((2, R, features), BF16),
        lots,
        dma((12,)),
        dma((2,)),
        dma((2,)),
        dma,
        dma,
        dma((swaps,)),
        dma((swaps,)),
        dma((2,)),
        dma((2,)),
    ]
    inputs = (
        grid_latent[0],
        hidden[0],
        d_updated[0],
        w_kv,
        w_q,
        src_gain.reshape(1, features),
        q_gain.reshape(1, features),
        src_index.T,
        edge_mask.T,
    )
    updated, d_grid, d_wkv_t = pl.pallas_call(
        functools.partial(layer_kernel, sizes, factor),
        out_shape=(
            jax.ShapeDtypeStruct((nodes, features), BF16),
            jax.ShapeDtypeStruct((rows, features), BF16),
            jax.ShapeDtypeStruct((own, features), F32),
        ),
        in_specs=[hbm] * 9,
        out_specs=(vmem, vmem, vmem),
        scratch_shapes=scratch,
        compiler_params=pltpu.CompilerParams(
            collective_id=0, has_side_effects=True, vmem_limit_bytes=52 * 1024 * 1024
        ),
        name="encoder_layer",
    )(
        *[pltpu.with_memory_space_constraint(value, pltpu.HBM) for value in inputs]
    )
    updated, d_grid, d_wkv_t = pl.pallas_call(
        leave_kernel,
        out_shape=(
            jax.ShapeDtypeStruct((nodes, features), BF16),
            jax.ShapeDtypeStruct((rows, features), BF16),
            jax.ShapeDtypeStruct((own, features), F32),
        ),
        in_specs=[vmem, vmem, vmem],
        out_specs=(hbm, hbm, hbm),
        scratch_shapes=[dma((3,))],
        compiler_params=pltpu.CompilerParams(vmem_limit_bytes=2 * 1024 * 1024),
        name="leave",
    )(updated, d_grid, d_wkv_t)
    return (updated[None], d_grid[None], d_wkv_t)


def solution(mesh):
    bands, members = mesh.shape["band"], mesh.shape["ens"]
    nx = 4
    nz = bands // (2 * nx)
    finer = Mesh(mesh.devices.reshape(nz, nx, 2, members), AXES)
    cells = P("ens", BAND, None)
    in_specs = (cells, cells, cells, P(), P(), P(), P(), P(BAND, None), P(BAND, None))
    out_specs = (cells, cells, P(AXES, None))
    return jax.shard_map(
        functools.partial(per_device, (nz, nx, members)),
        mesh=finer,
        in_specs=in_specs,
        out_specs=out_specs,
        check_vma=False,
    )
```

```python
import functools
import math

import jax
import jax.numpy as jnp
from jax import lax
from jax.experimental import pallas as pl
from jax.experimental.pallas import tpu as pltpu
from jax.sharding import Mesh
from jax.sharding import PartitionSpec as P

HEADS = 16
K = 12
R = 32
BAND = ("bz", "bx", "bc")
AXES = ("bz", "bx", "bc", "ens")
EPSILON = 1e-05
MESH = pl.DeviceIdType.MESH
F32 = jnp.float32
BF16 = jnp.bfloat16
LANES = 128
WIDTHS = (256, 256)


def dot(left, right, contract):
    return lax.dot_general(left, right, ((contract[:1], contract[1:]), ((), ())), preferred_element_type=F32)


def normalize(values):
    average = jnp.mean(values, axis=-1, keepdims=True)
    centred = values - average
    variance = jnp.mean(centred * centred, axis=-1, keepdims=True)
    inv_std = lax.rsqrt(variance + EPSILON)
    return centred * inv_std, inv_std


def layer_kernel(
    sizes,
    factor,
    grid_hbm,
    hidden_hbm,
    cot_hbm,
    wkv_hbm,
    wq_hbm,
    src_gain_hbm,
    q_gain_hbm,
    index_hbm,
    mask_hbm,
    updated_ref,
    dgrid_ref,
    dw_ref,
    grid_ref,
    hidden_ref,
    cot_ref,
    src_gain_ref,
    q_gain_ref,
    index_ref,
    mask_ref,
    edge,
    pairs,
    inner,
    wkv,
    wq,
    standard,
    inv_std,
    win,
    pair_win,
    kv,
    partial,
    parted,
    pair_parted,
    d_norm,
    back_send,
    back_recv,
    lots,
    load_sem,
    halo_send,
    halo_recv,
    win_send,
    win_recv,
    pair_send,
    pair_recv,
    back_ssem,
    back_rsem,
):
    nz, nx, ny = sizes
    nb = nz * nx * 2
    rows = grid_hbm.shape[0]
    nodes, features = hidden_hbm.shape
    window = rows + 2 * R
    half = features // 2
    own = dw_ref.shape[0]

    z, x = lax.axis_index("bz"), lax.axis_index("bx")
    c, y = lax.axis_index("bc"), lax.axis_index("ens")
    band = (z * nx + x) * 2 + c

    def of_band(b):
        return (b // (2 * nx), (b // 2) % nx, b % 2, y)

    below = of_band((band + nb - 1) % nb)
    above = of_band((band + 1) % nb)
    pair = (z, x, 1 - c, y)

    def x_peer(k):
        return (z, (x + k) % nx, c, y)

    def y_peer(k):
        return (z, x, c, (y + k) % ny)

    def z_peer(k):
        return ((z + k) % nz, x, c, y)

    def remote(src, dst, ssem, rsem, device):
        return pltpu.make_async_remote_copy(
            src_ref=src, dst_ref=dst, send_sem=ssem, recv_sem=rsem, device_id=device, device_id_type=MESH
        )

    def load(src, dst, i):
        copy = pltpu.make_async_copy(src, dst, load_sem.at[i])
        copy.start()
        return copy

    load_grid = load(grid_hbm, grid_ref, 0)
    barrier = pltpu.get_barrier_semaphore()
    greeted = [below, above]
    greeted += [x_peer(k) for k in range(1, nx)]
    greeted += [y_peer(k) for k in range(1, ny)]
    greeted += [z_peer(k) for k in range(1, nz)]
    for device in greeted:
        pl.semaphore_signal(barrier, inc=1, device_id=device, device_id_type=MESH)

    load_gain = load(src_gain_hbm, src_gain_ref, 1)
    load_hidden = load(hidden_hbm, hidden_ref, 2)
    load_q_gain = load(q_gain_hbm, q_gain_ref, 3)
    load_index = load(index_hbm, index_ref, 5)
    load_mask = load(mask_hbm, mask_ref, 6)
    load_cot = load(cot_hbm, cot_ref, 7)
    load_q = load(wq_hbm, wq, 4)
    quarter = [slice(j * half, (j + 1) * half) for j in range(4)]
    load_kv = [load(wkv_hbm.at[:, cols], wkv.at[:, cols], 8 + j) for j, cols in enumerate(quarter)]

    load_grid.wait()
    pl.semaphore_wait(barrier, len(greeted))

    halo = [
        remote(grid_ref.at[0:R], edge.at[1], halo_send.at[0], halo_recv.at[0], below),
        remote(grid_ref.at[rows - R : rows], edge.at[0], halo_send.at[1], halo_recv.at[1], above),
    ]
    for copy in halo:
        copy.start()

    load_gain.wait()
    hat, scale = normalize(grid_ref[...].astype(F32))
    standard[...] = hat
    inv_std[...] = scale
    win[:rows] = (hat * src_gain_ref[...]).astype(BF16)

    load_hidden.wait()
    load_q_gain.wait()
    hidden_hat, _ = normalize(hidden_ref[...].astype(F32))
    hidden_normed = (hidden_hat * q_gain_ref[...]).astype(BF16)
    load_q.wait()
    score_scale = 1.0 / math.sqrt(features // HEADS)
    queries = (dot(hidden_normed, wq[...], (1, 0)).astype(BF16).astype(F32) * score_scale).astype(BF16)

    load_index.wait()
    load_mask.wait()
    local = index_ref[...] - (band * rows - R)
    local = jnp.where(mask_ref[...] > 0, local, -1)
    row_ids = lax.broadcasted_iota(jnp.int32, (window, nodes), 0)
    row_ids = jnp.where(row_ids < rows, row_ids + R, jnp.where(row_ids < rows + R, row_ids - rows, row_ids))
    times = jnp.zeros((window, nodes), F32)
    for j in range(K):
        times = times + jnp.where(local[j : j + 1, :] == row_ids, 1.0, 0.0)
    times = times.T
    times = jnp.concatenate([times, times], axis=0)
    live = times > 0.0

    for j, cols in enumerate(quarter):
        load_kv[j].wait()
        kv[:rows, cols] = dot(win[:rows], wkv[:, cols], (1, 0)).astype(BF16)
    load_cot.wait()
    low_lane = lax.broadcasted_iota(jnp.int32, (nodes, LANES), 1) < features // HEADS
    cot = cot_ref[...]
    zero = jnp.zeros((nodes, LANES), F32)

    def two_heads(block):
        block = block.astype(F32)
        return jnp.concatenate(
            [jnp.where(low_lane, block, zero), jnp.where(low_lane, zero, block)], axis=0
        ).astype(BF16)

    def spans(j):
        return slice(j * LANES, (j + 1) * LANES), slice(features + j * LANES, features + (j + 1) * LANES)

    for j in range(features // LANES):
        span, vspan = spans(j)
        q2 = two_heads(queries[:, span])
        d2 = two_heads(cot[:, span])
        pairs[0, j], pairs[1, j] = q2, d2
        inner[0, j] = dot(q2, kv[:rows, span], (1, 1))
        inner[1, j] = dot(d2, kv[:rows, vspan], (1, 1))

    for copy in halo:
        copy.wait_recv()
    hat, _ = normalize(edge[...].reshape(2 * R, features).astype(F32))
    outer = (hat * src_gain_ref[...]).astype(BF16)
    win[rows:] = outer
    swap_win = remote(win, pair_win, win_send, win_recv, pair)
    swap_win.start()
    for cols in quarter:
        kv[rows:, cols] = dot(outer, wkv[:, cols], (1, 0)).astype(BF16)
    group = ny * own

    swaps = []

    def keep_parted(first, tile):
        piece = min(LANES, group)
        for i in range(LANES // piece):
            at, inside = divmod(first + i * piece, group)
            parted[at % 2, at // (2 * nx), at // 2 % nx, inside : inside + piece, :window] = tile[i * piece : (i + 1) * piece]

    def swap(first, count):
        n = len(swaps)
        swaps.append(
            remote(
                parted.at[1 - c, first : first + count],
                pair_parted.at[first : first + count],
                pair_send.at[n],
                pair_recv.at[n],
                pair,
            )
        )
        swaps[-1].start()

    batches = 2 if nz >= 4 else 1
    blocks = features // LANES
    planes = nz // (2 * batches)
    for batch in range(batches):
        mine = range(batch * blocks // batches, (batch + 1) * blocks // batches)
        q2s = [pairs[0, j] for j in mine]
        d2s = [pairs[1, j] for j in mine]
        scores = [
            jnp.concatenate([inner[0, j], dot(q2, kv[rows:, spans(j)[0]], (1, 1))], axis=1) for q2, j in zip(q2s, mine)
        ]
        d_probs = [
            jnp.concatenate([inner[1, j], dot(d2, kv[rows:, spans(j)[1]], (1, 1))], axis=1) for d2, j in zip(d2s, mine)
        ]
        weights, d_scores = [], []
        for score, d_prob in zip(scores, d_probs):
            shifted = jnp.where(live, score, -jnp.inf)
            terms = jnp.exp(shifted - jnp.max(shifted, axis=1, keepdims=True))
            probs = terms / jnp.sum(times * terms, axis=1, keepdims=True)
            weights.append((times * probs.astype(BF16).astype(F32)).astype(BF16))
            counted = times * probs
            d_scores.append((counted * (d_prob - jnp.sum(counted * d_prob, axis=1, keepdims=True))).astype(BF16))
        for j, q2, d2, weight, d_score in zip(mine, q2s, d2s, weights, d_scores):
            keep_parted(j * LANES, dot(q2, d_score, (0, 0)).astype(BF16))
            keep_parted(features + j * LANES, dot(d2, weight, (0, 0)).astype(BF16))
        swap(batch * planes, planes)
        swap(nz // 2 + batch * planes, planes)
        for j, q2, d2, weight, d_score in zip(mine, q2s, d2s, weights, d_scores):
            span, vspan = spans(j)
            mixed = dot(weight, kv[:, vspan], (1, 0))
            attended = jnp.where(low_lane, mixed[:nodes], mixed[nodes:])
            updated_ref[:, span] = (hidden_ref[:, span].astype(F32) + attended).astype(BF16)
            partial[:, span] = dot(d_score, q2, (0, 0)).astype(BF16)
            partial[:, vspan] = dot(weight, d2, (0, 0)).astype(BF16)

    swap_win.wait()
    for copy in swaps:
        copy.wait()

    def product(xd, cols):
        mine = jnp.concatenate([parted[c, i, xd, :, :window] for i in range(nz)], axis=0)
        other = jnp.concatenate([pair_parted[i, xd, :, :window] for i in range(nz)], axis=0)
        return dot(mine, win[:, cols], (1, 0)) + dot(other, pair_win[:, cols], (1, 0))

    starts = []
    left = 0
    for lot in lots:
        starts.append(left)
        left += lot["kept_a"].shape[-1]
    low, high = slice(0, nz // 2), slice(nz // 2, nz)

    def neighbours(lot, name, peer, piece):
        held, ssem, rsem = lot["recv_" + name], lot["ssem_" + name], lot["rsem_" + name]

        def forward(lot):
            over = lot["over_" + name]
            copies = [
                remote(piece(2).at[low], over.at[0], ssem.at[0], rsem.at[0], peer(1)),
                remote(piece(2).at[high], over.at[1], ssem.at[1], rsem.at[1], peer(3)),
            ]
            for copy in copies:
                copy.start()
            return copies

        def direct(k):
            i, part = (0, high) if k == 1 else (1, low)
            copy = remote(piece(k).at[part], held.at[i, part], ssem.at[2 + i], rsem.at[2 + i], peer(k))
            copy.start()
            return [copy]

        def augment(lot, forwards):
            over, copies = lot["over_" + name], []
            for i, (k, part) in enumerate([(1, low), (3, high)]):
                forwards[i].wait()
                target = piece(k).at[part]
                target[...] = (target[...].astype(F32) + over[i].astype(F32)).astype(BF16)
                copies.append(remote(target, held.at[i, part], ssem.at[4 + i], rsem.at[4 + i], peer(k)))
                copies[-1].start()
            return copies

        return forward, direct, augment

    first, augments = [], []
    for lot, start in zip(lots, starts):
        width = lot["kept_a"].shape[-1]
        send_a, send_b = lot["send_a"], lot["send_b"]
        forward_a, direct_a, augment_a = neighbours(lot, "a", x_peer, lambda k, ref=send_a: ref.at[k])
        forward_b, direct_b, augment_b = neighbours(lot, "b", y_peer, lambda k, ref=send_b: ref.at[(y + k) % ny])

        def x_piece(k):
            tile = product((x + k) % nx, slice(start, start + width))
            send_a[k] = tile.reshape(nz, ny, own, width).astype(BF16)

        x_piece(2)
        over_a = forward_a(lot)
        for xd in range(nx):
            tile = product(xd, slice(half + start, half + start + width))
            tile = tile.reshape(nz, ny, own, width).astype(BF16)
            for yd in range(ny):
                send_b[yd, :, xd] = tile[:, yd]
        over_b = forward_b(lot)
        copies_b = direct_b(1) + direct_b(3)
        x_piece(1)
        copies_a = direct_a(1)
        x_piece(3)
        copies_a += direct_a(3)
        x_piece(0)
        first.append((copies_a, copies_b))
        augments.append((augment_a, augment_b, over_a, over_b))

    def second_exchange(lot, copies_a, copies_b):
        sent_a, sent_b = [], []
        for copy in copies_b:
            copy.wait()
        for k in list(range(1, nx)) + [0]:
            xd = (x + k) % nx
            total = lot["send_b"][y, :, xd].astype(F32)
            for j in range(2):
                total = total + lot["recv_b"][j, :, xd].astype(F32)
            if k:
                i = k - 1
                lot["send_b2"][i] = total.astype(BF16)
                src, dst = lot["send_b2"].at[i], lot["recv_b2"].at[i]
                sent_b.append(remote(src, dst, lot["b2_ssem"].at[i], lot["b2_rsem"].at[i], x_peer(k)))
                sent_b[-1].start()
            else:
                lot["kept_b"][...] = total
        for copy in copies_a:
            copy.wait()
        for k in list(range(1, ny)) + [0]:
            yd = (y + k) % ny
            total = lot["send_a"][0, :, yd].astype(F32)
            for j in range(2):
                total = total + lot["recv_a"][j, :, yd].astype(F32)
            if k:
                i = k - 1
                lot["send_a2"][i] = total.astype(BF16)
                src, dst = lot["send_a2"].at[i], lot["recv_a2"].at[i]
                sent_a.append(remote(src, dst, lot["a2_ssem"].at[i], lot["a2_rsem"].at[i], y_peer(k)))
                sent_a[-1].start()
            else:
                lot["kept_a"][...] = total
        return sent_a, sent_b

    def third_exchange(lot, copies_a, copies_b):
        width = lot["kept_a"].shape[-1]
        send, sent = lot["send_z"], []
        for copy in copies_b:
            copy.wait()
        total = lot["kept_b"][...]
        for j in range(nx - 1):
            total = total + lot["recv_b2"][j].astype(F32)
        send[:, :, width:] = total.astype(BF16)
        for copy in copies_a:
            copy.wait()
        total = lot["kept_a"][...]
        for j in range(ny - 1):
            total = total + lot["recv_a2"][j].astype(F32)
        send[:, :, :width] = total.astype(BF16)
        for k in sorted(range(1, nz), key=lambda k: abs(2 * k - nz)):
            i, src = k - 1, send.at[(z + k) % nz]
            sent.append(remote(src, lot["recv_z"].at[i], lot["z_ssem"].at[i], lot["z_rsem"].at[i], z_peer(k)))
            sent[-1].start()
        return sent

    for lot, (augment_a, augment_b, over_a, over_b), (copies_a, copies_b) in zip(lots, augments, first):
        copies_a += augment_a(lot, over_a)
        copies_b += augment_b(lot, over_b)

    second = [second_exchange(lots[0], *first[0])]

    for lot, copies in zip(lots[1:], first[1:]):
        second.append(second_exchange(lot, *copies))
    part = partial[...]
    for j in range(2):
        cols = pl.ds(j * half, half)
        d_norm[:, cols] = dot(part, wkv[cols, :], (1, 1))
    back_send[0] = d_norm[rows : rows + R].astype(BF16)
    back_send[1] = d_norm[rows + R : window].astype(BF16)
    back = [
        remote(back_send.at[0], back_recv.at[0], back_ssem.at[0], back_rsem.at[0], below),
        remote(back_send.at[1], back_recv.at[1], back_ssem.at[1], back_rsem.at[1], above),
    ]
    for copy in back:
        copy.start()
    third = [third_exchange(lot, *copies) for lot, copies in zip(lots, second)]
    for copy in back:
        copy.wait()
    d_norm[:R] += back_recv[1].astype(F32)
    d_norm[rows - R : rows] += back_recv[0].astype(F32)
    dx = d_norm[:rows] * src_gain_ref[...]
    hat = standard[...]
    dgrid_ref[...] = (
        inv_std[...]
        * (dx - jnp.mean(dx, axis=-1, keepdims=True) - hat * jnp.mean(dx * hat, axis=-1, keepdims=True))
    ).astype(BF16)


    for lot, start, copies in zip(lots, starts, third):
        width = lot["kept_a"].shape[-1]
        total = lot["send_z"][z].astype(F32)
        for copy in copies:
            copy.wait()
        for k in range(1, nz):
            total = total + lot["recv_z"][k - 1].astype(F32)
        total = total * factor
        dw_ref[:, start : start + width] = total[:, :width]
        dw_ref[:, half + start : half + start + width] = total[:, width:]
    for copy in halo:
        copy.wait_send()


def leave_kernel(a, b, c, a_out, b_out, c_out, sem):
    copies = [
        pltpu.make_async_copy(src, dst, sem.at[i])
        for i, (src, dst) in enumerate([(b, b_out), (a, a_out), (c, c_out)])
    ]
    for copy in copies:
        copy.start()
    for copy in copies:
        copy.wait()


def per_device(sizes, grid_latent, hidden, d_updated, w_kv, w_q, src_gain, q_gain, src_index, edge_mask):
    nz, nx, ny = sizes
    _, rows, features = grid_latent.shape
    nodes = hidden.shape[1]
    window = rows + 2 * R
    half = features // 2
    columns = w_kv.shape[1]
    own = columns // (nz * nx * 2 * ny)
    factor = 1.0 / math.sqrt(ny * rows * nz * nx * 2)
    vmem = pl.BlockSpec(memory_space=pltpu.VMEM)
    hbm = pl.BlockSpec(memory_space=pltpu.HBM)
    dma = pltpu.SemaphoreType.DMA
    V = pltpu.VMEM
    padded = -(-window // LANES) * LANES
    swaps = 4 if nz >= 4 else 2
    lots = []
    for width in WIDTHS:
        lots.append(
            dict(
                send_a=V((nx, nz, ny, own, width), BF16),
                recv_a=V((2, nz, ny, own, width), BF16),
                over_a=V((2, nz // 2, ny, own, width), BF16),
                send_b=V((ny, nz, nx, own, width), BF16),
                recv_b=V((2, nz, nx, own, width), BF16),
                over_b=V((2, nz // 2, nx, own, width), BF16),
                send_a2=V((ny - 1, nz, own, width), BF16),
                recv_a2=V((ny - 1, nz, own, width), BF16),
                send_b2=V((nx - 1, nz, own, width), BF16),
                recv_b2=V((nx - 1, nz, own, width), BF16),
                kept_a=V((nz, own, width), F32),
                kept_b=V((nz, own, width), F32),
                send_z=V((nz, own, 2 * width), BF16),
                recv_z=V((nz - 1, own, 2 * width), BF16),
                ssem_a=dma((6,)),
                rsem_a=dma((6,)),
                ssem_b=dma((6,)),
                rsem_b=dma((6,)),
                a2_ssem=dma((ny - 1,)),
                a2_rsem=dma((ny - 1,)),
                b2_ssem=dma((nx - 1,)),
                b2_rsem=dma((nx - 1,)),
                z_ssem=dma((nz - 1,)),
                z_rsem=dma((nz - 1,)),
            )
        )
    scratch = [
        V((rows, features), BF16),
        V((nodes, features), BF16),
        V((nodes, features), BF16),
        V((1, features), F32),
        V((1, features), F32),
        V((K, nodes), jnp.int32),
        V((K, nodes), jnp.int32),
        V((2, R, features), BF16),
        V((2, features // LANES, 2 * nodes, LANES), BF16),
        V((2, features // LANES, 2 * nodes, rows), F32),
        V((features, columns), BF16),
        V((features, features), BF16),
        V((rows, features), F32),
        V((rows, 1), F32),
        V((window, features), BF16),
        V((window, features), BF16),
        V((window, columns), BF16),
        V((window, columns), BF16),
        V((2, nz, nx, ny * own, padded), BF16),
        V((nz, nx, ny * own, padded), BF16),
        V((window, features), F32),
        V((2, R, features), BF16),
        V((2, R, features), BF16),
        lots,
        dma((12,)),
        dma((2,)),
        dma((2,)),
        dma,
        dma,
        dma((swaps,)),
        dma((swaps,)),
        dma((2,)),
        dma((2,)),
    ]
    inputs = (
        grid_latent[0],
        hidden[0],
        d_updated[0],
        w_kv,
        w_q,
        src_gain.reshape(1, features),
        q_gain.reshape(1, features),
        src_index.T,
        edge_mask.T,
    )
    updated, d_grid, d_wkv_t = pl.pallas_call(
        functools.partial(layer_kernel, sizes, factor),
        out_shape=(
            jax.ShapeDtypeStruct((nodes, features), BF16),
            jax.ShapeDtypeStruct((rows, features), BF16),
            jax.ShapeDtypeStruct((own, features), F32),
        ),
        in_specs=[hbm] * 9,
        out_specs=(vmem, vmem, vmem),
        scratch_shapes=scratch,
        compiler_params=pltpu.CompilerParams(
            collective_id=0, has_side_effects=True, vmem_limit_bytes=52 * 1024 * 1024
        ),
        name="encoder_layer",
    )(
        *[pltpu.with_memory_space_constraint(value, pltpu.HBM) for value in inputs]
    )
    updated, d_grid, d_wkv_t = pl.pallas_call(
        leave_kernel,
        out_shape=(
            jax.ShapeDtypeStruct((nodes, features), BF16),
            jax.ShapeDtypeStruct((rows, features), BF16),
            jax.ShapeDtypeStruct((own, features), F32),
        ),
        in_specs=[vmem, vmem, vmem],
        out_specs=(hbm, hbm, hbm),
        scratch_shapes=[dma((3,))],
        compiler_params=pltpu.CompilerParams(vmem_limit_bytes=2 * 1024 * 1024),
        name="leave",
    )(updated, d_grid, d_wkv_t)
    return (updated[None], d_grid[None], d_wkv_t)


def solution(mesh):
    bands, members = mesh.shape["band"], mesh.shape["ens"]
    nx = 4
    nz = bands // (2 * nx)
    finer = Mesh(mesh.devices.reshape(nz, nx, 2, members), AXES)
    cells = P("ens", BAND, None)
    in_specs = (cells, cells, cells, P(), P(), P(), P(), P(BAND, None), P(BAND, None))
    out_specs = (cells, cells, P(AXES, None))
    return jax.shard_map(
        functools.partial(per_device, (nz, nx, members)),
        mesh=finer,
        in_specs=in_specs,
        out_specs=out_specs,
        check_vma=False,
    )
```
